512 devices in a mesh: dp: 16 (over z, core), table: 32 (over y, x).
Axes of the slice: x: 4, y: 8, z: 8, core: 2. Of those that a mesh axis runs over, the one named last changes fastest.
Arguments:
- table: bfloat16 [16384, 256], P('table'), may hold values from -6 to 6
- weights: bfloat16 [2, 6, 256, 256], replicated, may hold values from -0.375 to 0.375
- fetch_rows: int32 [16, 32, 32, 32], P('dp', 'table'), may hold values from 0 to 511
- fetch_count: int32 [16, 32, 32], P('dp', 'table'), may hold values from 1 to 32, as said below
- first_self: int32 [16, 32, 256], P('dp', 'table'), may hold values from 0 to 1023, as said below
- first_edges: int32 [16, 32, 5, 256, 4], P('dp', 'table'), may hold values from 0 to 1023, as said below
- first_degree: int32 [16, 32, 5, 256], P('dp', 'table'), may hold values from 1 to 4
- second_self: int32 [16, 32, 128], P('dp', 'table'), may hold values from 0 to 255
- second_edges: int32 [16, 32, 5, 128, 4], P('dp', 'table'), may hold values from 0 to 255
- second_degree: int32 [16, 32, 5, 128], P('dp', 'table'), may hold values from 1 to 4
- cotangent: bfloat16 [16, 32, 128, 256], P('dp', 'table'), may hold values from -6 to 6
Outputs:
- node_out: bfloat16 [16, 32, 128, 256], P('dp', 'table')
- weight_grad: bfloat16 [2, 6, 256, 256], replicated
- table_grad: float32 [32, 512, 256], P('table', 'dp')
The draws below stay inside these ranges and needn't reach their ends.
Inputs may be any that keep to these rules, and one draw needn't show every extreme that they name: Minibatch (i, j) uses the first fetch_count[i, j, k] slots for shard k; for each i one shard is given all 32 slots by every minibatch of that i, and every other count is at most 16. `fetch_rows`: slots past the count hold arbitrary row numbers. `first_self`: every entry is a live slot k * 32 + c with c < fetch_count of shard k. `first_edges`: every entry, used or not, is a live slot k * 32 + c with c < fetch_count of shard k.
All inputs are finite; a program needn't handle non-finite values.
Results may differ from the reference program's by a relative error of at most 0.0057.
Values may be sent and summed in bfloat16 or wider, within the bound.
No kernel may reach another device: no remote copies, remote signals or barrier semaphores. Data moves between devices by JAX's collectives and lax.ppermute only.
A program may use at most 64 MiB of HBM per device.

```python
import jax
import jax.numpy as jnp
from jax import lax

D = 256
R = 5
FAN = 4
ROWS_DEV = 512
CAP = 32
B2 = 128
B1 = 256
SLOTS = 1024
VOCAB = 16384
SEEDS = 65536
N_DP = 16
N_TABLE = 32


def owner_counts(key):
    layout = (N_DP, N_TABLE, N_TABLE)
    lowest = max(1, CAP // 8)
    drawn = jax.random.randint(jax.random.fold_in(key, 11), layout, lowest, CAP // 2 + 1)
    hottest = jax.random.randint(jax.random.fold_in(key, 12), (N_DP, 1, 1), 0, N_TABLE)
    owners = lax.broadcasted_iota(jnp.int32, layout, 2)
    return jnp.where(owners == hottest, CAP, drawn).astype(jnp.int32)


def live_slots(key, extent, salt):
    counts = owner_counts(key)
    owners = jax.random.randint(jax.random.fold_in(key, salt), extent, 0, N_TABLE)
    flatwise = owners.reshape(N_DP, N_TABLE, -1)
    limits = jnp.take_along_axis(counts, flatwise, axis=2).reshape(extent)
    within = jax.random.randint(jax.random.fold_in(key, salt + 1), extent, 0, limits)
    return (owners * CAP + within).astype(jnp.int32)


def draw_fetch_count(key, part):
    return owner_counts(key)


def draw_first_self(key, part):
    return live_slots(key, (N_DP, N_TABLE, B1), 21)


def draw_first_edges(key, part):
    return live_slots(key, (N_DP, N_TABLE, R, B1, FAN), 31)


def plant(values, own_key, smallest, high):
    longest = values.shape.index(max(values.shape))
    spots = []
    for shift in (0, 1):
        where = [jax.random.randint(jax.random.fold_in(own_key, axis), (), 0, length) for axis, length in enumerate(values.shape)]
        where[longest] = (where[longest] + shift) % values.shape[longest]
        spots.append(tuple(where))
    return values.at[spots[0]].set(smallest).at[spots[1]].set(high)


def steps_of(key, shape, split, low, high):
    loudness = 1.0
    for dim, blocks in split:
        heights = jax.random.uniform(jax.random.fold_in(jax.random.fold_in(key, 6), dim), (blocks,), jnp.float32, low / len(split), high / len(split))
        loudness = loudness * jnp.repeat(jnp.exp(heights), shape[dim] // blocks).reshape((-1,) + (1,) * (len(shape) - 1 - dim))
    return loudness


def centred(own_key, shape, width, limit, split=(), kind=jnp.bfloat16):
    entries = jax.random.normal(own_key, shape, jnp.float32) * width
    if len(split) > 0:
        entries = steps_of(own_key, shape, split, -0.22, 0.18) * entries
    return jnp.clip(entries, min=-limit, max=limit).astype(kind)


def setup_inputs(seed: int = 0) -> dict:
    keys = jax.random.split(jax.random.key(seed), 12)
    table = centred(keys[0], (VOCAB, D), 1.0, 6.0, ((0, 32),))
    weights = centred(keys[1], (2, R + 1, D, D), D ** -0.5, 0.375)
    fetch_rows = plant(jax.random.randint(keys[2], (N_DP, N_TABLE, N_TABLE, CAP), 0, ROWS_DEV), jax.random.fold_in(keys[2], 1), 0, ROWS_DEV - 1).astype(jnp.int32)
    fetch_count = draw_fetch_count(jax.random.fold_in(keys[11], 71), 0)
    first_self = draw_first_self(jax.random.fold_in(keys[11], 71), 0)
    first_edges = draw_first_edges(jax.random.fold_in(keys[11], 71), 0)
    first_degree = plant(jax.random.randint(keys[6], (N_DP, N_TABLE, R, B1), 1, FAN + 1), jax.random.fold_in(keys[6], 1), 1, FAN).astype(jnp.int32)
    second_self = plant(jax.random.randint(keys[7], (N_DP, N_TABLE, B2), 0, B1), jax.random.fold_in(keys[7], 1), 0, B1 - 1).astype(jnp.int32)
    second_edges = plant(jax.random.randint(keys[8], (N_DP, N_TABLE, R, B2, FAN), 0, B1), jax.random.fold_in(keys[8], 1), 0, B1 - 1).astype(jnp.int32)
    second_degree = plant(jax.random.randint(keys[9], (N_DP, N_TABLE, R, B2), 1, FAN + 1), jax.random.fold_in(keys[9], 1), 1, FAN).astype(jnp.int32)
    cotangent = centred(keys[10], (N_DP, N_TABLE, B2, D), 1.0, 6.0, ((0, 16), (1, 32)))
    return dict(table=table, weights=weights, fetch_rows=fetch_rows, fetch_count=fetch_count, first_self=first_self, first_edges=first_edges, first_degree=first_degree, second_self=second_self, second_edges=second_edges, second_degree=second_degree, cotangent=cotangent)


def aggregate(features, edges, degrees):

    def single(bundle):
        indices, degree = bundle
        within = lax.broadcasted_iota(jnp.int32, indices.shape, 1) < degree[:, None]
        picked = jnp.where(within[:, :, None], features[indices], jnp.zeros((), features.dtype))
        summed = lax.optimization_barrier(jnp.sum(picked.astype(jnp.float32), axis=1))
        return (summed / degree[:, None].astype(jnp.float32)).astype(jnp.bfloat16)
    return lax.map(single, (edges, degrees))

def spread_back(grads, edges, degrees, height):

    def single(running, bundle):
        part_grad, indices, degree = bundle
        within = lax.broadcasted_iota(jnp.int32, indices.shape, 1) < degree[:, None]
        scaled = part_grad / degree[:, None].astype(part_grad.dtype)
        placed = jnp.where(within[:, :, None], scaled[:, None, :], jnp.zeros((), part_grad.dtype))
        return (running.at[indices.reshape(-1)].add(placed.reshape(-1, part_grad.shape[-1])), None)
    initial = jnp.zeros((height, grads.shape[-1]), grads.dtype)
    result, ignored = lax.scan(single, initial, (grads, edges, degrees))
    return result

def relation_sum(agg, layer_weights):
    return jnp.einsum('rbd,rde->be', agg.astype(jnp.float32), layer_weights.astype(jnp.float32))

def silu_slope(preact):
    logistic = jax.nn.sigmoid(preact)
    return logistic * (1.0 + preact * (1.0 - logistic))

def weight_terms(own_rows, agg, grad):
    own_term = lax.dot_general(own_rows, grad, (((0,), (0,)), ((), ())), preferred_element_type=jnp.float32)
    rel_terms = jnp.einsum('rbd,be->rde', agg.astype(jnp.float32), grad.astype(jnp.float32))
    return jnp.concatenate([own_term[None], rel_terms], axis=0)

def input_terms(grad, layer_weights):
    own_back = lax.dot_general(grad, layer_weights[0], (((1,), (1,)), ((), ())), preferred_element_type=jnp.float32)
    rel_back = jnp.einsum('be,rde->rbd', grad.astype(jnp.float32), layer_weights[1:].astype(jnp.float32))
    return (own_back, rel_back)

def sage_step(inputs, weights, first_self, first_edges, first_degree, second_self, second_edges, second_degree, cotangent):
    first_agg = aggregate(inputs, first_edges, first_degree)
    first_own = inputs[first_self]
    first_pre = jnp.dot(first_own, weights[0, 0], preferred_element_type=jnp.float32) + relation_sum(first_agg, weights[0, 1:])
    hidden = jax.nn.silu(first_pre).astype(jnp.bfloat16)
    second_agg = aggregate(hidden, second_edges, second_degree)
    second_own = hidden[second_self]
    output = jnp.dot(second_own, weights[1, 0], preferred_element_type=jnp.float32) + relation_sum(second_agg, weights[1, 1:])
    grad_top = weight_terms(second_own, second_agg, cotangent)
    own_back, rel_back = input_terms(cotangent, weights[1])
    grad_hidden = jnp.zeros((hidden.shape[0], hidden.shape[1]), jnp.float32).at[second_self].add(own_back)
    grad_hidden = grad_hidden + spread_back(rel_back, second_edges, second_degree, hidden.shape[0])
    grad_pre = (grad_hidden * silu_slope(first_pre)).astype(jnp.bfloat16)
    grad_bottom = weight_terms(first_own, first_agg, grad_pre)
    own_back, rel_back = input_terms(grad_pre, weights[0])
    grad_slots = jnp.zeros((inputs.shape[0], inputs.shape[1]), jnp.float32).at[first_self].add(own_back)
    grad_slots = grad_slots + spread_back(rel_back, first_edges, first_degree, inputs.shape[0])
    return (output.astype(jnp.bfloat16), jnp.stack([grad_bottom, grad_top]), grad_slots)

def reference(table, weights, fetch_rows, fetch_count, first_self, first_edges, first_degree, second_self, second_edges, second_degree, cotangent):
    batches = N_DP * N_TABLE

    def flatten(array):
        return array.reshape((batches,) + array.shape[2:])
    shard_rows = table.reshape(N_TABLE, ROWS_DEV, D)

    def single(carry, bundle):
        wanted, live_count, s_one, e_one, d_one, s_two, e_two, d_two, cot_rows = bundle
        slot_pos = lax.broadcasted_iota(jnp.int32, wanted.shape, 1)
        owners = lax.broadcasted_iota(jnp.int32, wanted.shape, 0)
        living = slot_pos < live_count[:, None]
        fetched = jnp.where(living[:, :, None], shard_rows[owners, wanted], jnp.zeros((), table.dtype))
        inputs = fetched.reshape(SLOTS, D)
        node_rows, grads, grad_slots = sage_step(inputs, weights, s_one, e_one, d_one, s_two, e_two, d_two, cot_rows)
        grad_slots = jnp.where(living.reshape(-1)[:, None], grad_slots, jnp.zeros((), grad_slots.dtype))
        weight_total, table_total = carry
        targets = (owners * ROWS_DEV + wanted).reshape(-1).astype(jnp.int32)
        table_total = table_total.at[targets].add(grad_slots)
        return ((weight_total + grads, table_total), node_rows)
    initial = (jnp.zeros((2, R + 1, D, D), jnp.float32), jnp.zeros((VOCAB, D), jnp.float32))
    bundles = tuple((flatten(a) for a in (fetch_rows, fetch_count, first_self, first_edges, first_degree, second_self, second_edges, second_degree, cotangent)))
    (weight_total, table_total), outputs = lax.scan(single, initial, bundles)
    node_out = outputs.reshape(N_DP, N_TABLE, B2, D)
    weight_grad = (weight_total / jnp.sqrt(jnp.float32(SEEDS))).astype(jnp.bfloat16)
    table_grad = table_total.reshape(N_TABLE, ROWS_DEV, D)
    return (node_out, weight_grad, table_grad)
```

```python
import jax
import jax.numpy as jnp
from jax import lax
from jax.experimental import pallas as pl
from jax.experimental.pallas import tpu as pltpu
from jax.sharding import PartitionSpec as P

BF = jnp.bfloat16
F32 = jnp.float32
PARAMS = pltpu.CompilerParams(vmem_limit_bytes=48 * 1024 * 1024)


def dot(a, b):
    return lax.dot_general(a, b, (((1,), (0,)), ((), ())), preferred_element_type=F32)


def dot_nt(a, b):
    return lax.dot_general(a, b, (((1,), (1,)), ((), ())), preferred_element_type=F32)


def two_part(x):
    high = x.astype(BF)
    return high, (x - high.astype(F32)).astype(BF)


def gather_kernel(asked_ref, table_ref, out_ref, hot_ref):
    groups, width = asked_ref.shape
    rows = table_ref.shape[0]
    columns = jnp.transpose(asked_ref[...].astype(F32))
    lanes = lax.broadcasted_iota(jnp.int32, (width, rows), 1).astype(F32)
    for j in range(groups):
        hot_ref[pl.ds(j * width, width), :] = jnp.where(
            lanes == columns[:, j : j + 1], 1.0, 0.0
        ).astype(BF)
    out_ref[...] = dot(hot_ref[...], table_ref[...]).astype(BF)


def counts_of(selfs, edges_ref, degree_ref, out_ref, height):
    relations, fan, nodes = edges_ref.shape
    slots = lax.broadcasted_iota(jnp.int32, (height, nodes), 0)
    out_ref[:, 0:nodes] = jnp.where(slots == selfs, 1.0, 0.0).astype(BF)
    for r in range(relations):
        degree = degree_ref[r : r + 1, :]
        total = None
        for f in range(fan):
            edge = jnp.where(degree > f, edges_ref[r, f : f + 1, :], -1)
            hit = jnp.where(slots == edge, 1.0, 0.0)
            total = hit if total is None else total + hit
        out_ref[:, (r + 1) * nodes : (r + 2) * nodes] = total.astype(BF)


def inverse_columns(degree_ref):
    relations, nodes = degree_ref.shape
    inverse = 1.0 / degree_ref[...].astype(F32)
    padded = jnp.concatenate([inverse, jnp.ones((8 - relations, nodes), F32)], axis=0)
    return jnp.transpose(padded)


def prepare_kernel(
    self1_ref,
    edges1_ref,
    degree1_ref,
    self2_ref,
    edges2_ref,
    degree2_ref,
    weights_ref,
    cot_ref,
    m1_ref,
    m2_ref,
    wt_ref,
    back_ref,
    column_ref,
    high_ref,
    low_ref,
):
    counts_of(self1_ref[...], edges1_ref, degree1_ref, m1_ref, m1_ref.shape[0])
    counts_of(self2_ref[...], edges2_ref, degree2_ref, m2_ref, m2_ref.shape[0])
    layers, kinds = weights_ref.shape[0], weights_ref.shape[1]
    for layer in range(layers):
        for r in range(kinds):
            wt_ref[layer, r] = jnp.transpose(weights_ref[layer, r].astype(F32)).astype(BF)
    column_ref[...] = inverse_columns(degree1_ref)
    column2 = inverse_columns(degree2_ref)
    seeds = cot_ref.shape[0]
    cot = cot_ref[...]
    for r in range(kinds):
        part = dot_nt(cot, weights_ref[1, r])
        if r > 0:
            part = part * column2[:, r - 1 : r]
        high, low = two_part(part)
        high_ref[pl.ds(r * seeds, seeds), :] = high
        low_ref[pl.ds(r * seeds, seeds), :] = low
    m2 = m2_ref[...]
    back_ref[...] = jnp.transpose(dot(m2, high_ref[...]) + dot(m2, low_ref[...]))


def main_kernel(
    count_ref,
    core_ref,
    x_ref,
    m1_ref,
    m2_ref,
    wt_ref,
    back_ref,
    column_ref,
    degree1_ref,
    degree2_ref,
    cot_ref,
    node_ref,
    slot_ref,
    keep_ref,
    send_ref,
    live_ref,
    agg_ref,
    agg2_ref,
    spread_ref,
):
    shards = count_ref.shape[1]
    slots, feature = x_ref.shape
    width = slots // shards
    kinds = wt_ref.shape[1]
    nodes = degree1_ref.shape[1]
    seeds = degree2_ref.shape[1]
    position = lax.broadcasted_iota(jnp.int32, (width, feature), 0)
    for k in range(shards):
        rows = x_ref[pl.ds(k * width, width), :].astype(F32)
        live_ref[pl.ds(k * width, width), :] = jnp.where(position < count_ref[0, k], rows, 0.0)
    xt = jnp.transpose(live_ref[...]).astype(BF)
    inverse1 = 1.0 / degree1_ref[...].astype(F32)
    inverse2 = 1.0 / degree2_ref[...].astype(F32)
    pre = None
    for r in range(kinds):
        part = dot(xt, m1_ref[:, r * nodes : (r + 1) * nodes])
        if r > 0:
            part = part * inverse1[r - 1 : r, :]
        part = part.astype(BF)
        agg_ref[:, r * nodes : (r + 1) * nodes] = part
        term = dot(wt_ref[0, r], part)
        pre = term if pre is None else pre + term
    logistic = 1.0 / (1.0 + jnp.exp(-pre))
    hidden = (pre * logistic).astype(BF)
    slope = logistic * (1.0 + pre * (1.0 - logistic))
    grad_pre = jnp.transpose(back_ref[...] * slope).astype(BF)
    out = None
    for r in range(kinds):
        part = dot(hidden, m2_ref[:, r * seeds : (r + 1) * seeds])
        if r > 0:
            part = part * inverse2[r - 1 : r, :]
        part = part.astype(BF)
        agg2_ref[:, r * seeds : (r + 1) * seeds] = part
        term = dot(wt_ref[1, r], part)
        out = term if out is None else out + term
    node_ref[...] = jnp.transpose(out).astype(BF)
    for r in range(kinds):
        part = dot(grad_pre, wt_ref[0, r])
        if r > 0:
            part = part * column_ref[:, r - 1 : r]
        spread_ref[pl.ds(r * nodes, nodes), :] = part.astype(BF)
    live_ref[...] = dot(m1_ref[...], spread_ref[...])
    for k in range(shards):
        rows = live_ref[pl.ds(k * width, width), :]
        slot_ref[pl.ds(k * width, width), :] = jnp.where(
            position < count_ref[0, k], rows, 0.0
        ).astype(BF)

    def bottom(r):
        return dot(agg_ref[:, r * nodes : (r + 1) * nodes], grad_pre)

    def top(r):
        return dot(agg2_ref[:, r * seeds : (r + 1) * seeds], cot_ref[...])

    @pl.when(core_ref[0] == 0)
    def first():
        for r in range(kinds):
            keep_ref[r] = bottom(r)
            send_ref[r] = top(r).astype(BF)

    @pl.when(core_ref[0] != 0)
    def second():
        for r in range(kinds):
            keep_ref[r] = top(r)
            send_ref[r] = bottom(r).astype(BF)


def scatter_kernel(asked_ref, back_ref, core_ref, out_ref):
    shards, height, feature = back_ref.shape
    groups, piece = out_ref.shape[0], out_ref.shape[1]
    width = asked_ref.shape[1] // shards
    rows = 512
    share = rows // groups
    grads = back_ref[:, 0:width, :].reshape(shards * width, feature)
    index = lax.broadcasted_iota(jnp.int32, (rows, shards * width), 0)
    hot = jnp.where(index == asked_ref[...], 1.0, 0.0).astype(BF)
    dense = dot(hot, grads)
    out_ref[:, 0:share, :] = dense.reshape(groups, share, feature).astype(BF)


def whole(n):
    return [pl.BlockSpec(memory_space=pltpu.VMEM)] * n


def shaped(shape, kind):
    return jax.ShapeDtypeStruct(shape, kind)


def body(
    table,
    weights,
    fetch_rows,
    fetch_count,
    first_self,
    first_edges,
    first_degree,
    second_self,
    second_edges,
    second_degree,
    cotangent,
):
    wanted = fetch_rows[0, 0]
    shards, width = wanted.shape
    rows, feature = table.shape
    slots = shards * width
    kinds = weights.shape[1]
    nodes = first_self.shape[2]
    seeds = second_self.shape[2]
    groups = lax.axis_size("dp")
    chips = groups // 2
    core = lax.axis_index("dp") % 2
    swap = [(i, i ^ 1) for i in range(groups)]
    lines = [[c + 2 * z for z in range(chips)] for c in range(2)]
    smem = pl.BlockSpec(memory_space=pltpu.SMEM)

    asked = lax.all_to_all(wanted, "table", split_axis=0, concat_axis=0, tiled=True)

    degree1 = first_degree[0, 0]
    degree2 = second_degree[0, 0]
    cot = cotangent[0, 0]
    m1, m2, wt, back, column = pl.pallas_call(
        prepare_kernel,
        out_shape=(
            shaped((slots, kinds * nodes), BF),
            shaped((nodes, kinds * seeds), BF),
            shaped(weights.shape, BF),
            shaped((feature, nodes), F32),
            shaped((nodes, 8), F32),
        ),
        in_specs=whole(8),
        out_specs=tuple(whole(5)),
        scratch_shapes=[
            pltpu.VMEM((kinds * seeds, feature), BF),
            pltpu.VMEM((kinds * seeds, feature), BF),
        ],
        compiler_params=PARAMS,
        name="prepare",
    )(
        first_self[0],
        jnp.swapaxes(first_edges[0, 0], 1, 2),
        degree1,
        second_self[0],
        jnp.swapaxes(second_edges[0, 0], 1, 2),
        degree2,
        weights,
        cot,
    )

    found = pl.pallas_call(
        gather_kernel,
        out_shape=shaped((slots, feature), BF),
        in_specs=whole(2),
        out_specs=whole(1)[0],
        scratch_shapes=[pltpu.VMEM((slots, rows), BF)],
        compiler_params=PARAMS,
        name="gather",
    )(asked, table)
    inputs = lax.all_to_all(found, "table", split_axis=0, concat_axis=0, tiled=True)

    node_out, slot_grads, keep, send = pl.pallas_call(
        main_kernel,
        out_shape=(
            shaped((seeds, feature), BF),
            shaped((slots, feature), BF),
            shaped((kinds, feature, feature), F32),
            shaped((kinds, feature, feature), BF),
        ),
        in_specs=[smem, smem] + whole(9),
        out_specs=tuple(whole(4)),
        scratch_shapes=[
            pltpu.VMEM((slots, feature), F32),
            pltpu.VMEM((feature, kinds * nodes), BF),
            pltpu.VMEM((feature, kinds * seeds), BF),
            pltpu.VMEM((kinds * nodes, feature), BF),
        ],
        compiler_params=PARAMS,
        name="step",
    )(
        fetch_count[0],
        core.reshape(1),
        inputs,
        m1,
        m2,
        wt,
        back,
        column,
        degree1,
        degree2,
        cot,
    )

    other = lax.ppermute(send, "dp", swap)
    half = (keep + other.astype(F32)).astype(BF)
    joined = jnp.concatenate(
        [slot_grads.reshape(shards, width, feature), half.reshape(shards, -1, feature)], axis=1
    )
    returned = lax.all_to_all(joined, "table", split_axis=0, concat_axis=0, tiled=True)

    share = rows // groups
    dense = pl.pallas_call(
        scatter_kernel,
        out_shape=shaped((groups, share, feature), BF),
        in_specs=whole(2) + [smem],
        out_specs=whole(1)[0],
        compiler_params=PARAMS,
        name="scatter",
    )(asked.reshape(1, slots), returned, core.reshape(1))
    partial = jnp.sum(returned[:, width:, :].astype(F32), axis=0)
    part_high, part_low = two_part(partial)
    parts = jnp.concatenate(
        [part_high.reshape(chips, 1, -1, feature), part_low.reshape(chips, 1, -1, feature)], axis=2
    )
    mine = lax.broadcasted_iota(jnp.int32, (1, 2, 1, 1), 1) == core
    parts = jnp.where(mine, parts, jnp.zeros((), BF)).reshape(groups, -1, feature)
    crossed = lax.all_to_all(
        jnp.concatenate([dense, parts], axis=1), "dp", split_axis=0, concat_axis=0, tiled=True
    )
    summed = jnp.sum(crossed.astype(F32), axis=0)
    table_part = summed[:share]
    piece = (summed.shape[0] - share) // 2
    total = summed[share : share + piece] + summed[share + piece :]
    batch = seeds * groups * shards
    mean = (total / jnp.sqrt(jnp.float32(batch))).astype(BF)
    stack = lax.all_to_all(
        jnp.broadcast_to(mean[None], (chips, piece, feature)).reshape(-1, feature),
        "dp",
        split_axis=0,
        concat_axis=0,
        tiled=True,
        axis_index_groups=lines,
    )
    mine_half = lax.all_to_all(
        jnp.broadcast_to(stack[None], (shards,) + stack.shape).reshape(-1, feature),
        "table",
        split_axis=0,
        concat_axis=0,
        tiled=True,
    ).reshape(kinds, feature, feature)
    other_half = lax.ppermute(mine_half, "dp", swap)
    weight_grad = jnp.stack(
        [
            jnp.where(core == 0, mine_half, other_half),
            jnp.where(core == 0, other_half, mine_half),
        ]
    )
    return (node_out[None, None], weight_grad, table_part[None])


def solution(mesh):
    return jax.shard_map(
        body,
        mesh=mesh,
        in_specs=(
            P("table", None),
            P(),
            P("dp", "table", None, None),
            P("dp", "table", None),
            P("dp", "table", None),
            P("dp", "table", None, None, None),
            P("dp", "table", None, None),
            P("dp", "table", None),
            P("dp", "table", None, None, None),
            P("dp", "table", None, None),
            P("dp", "table", None, None),
        ),
        out_specs=(P("dp", "table", None, None), P(), P("table", "dp", None)),
        check_vma=False,
    )
```

```python
import jax
import jax.numpy as jnp
from jax import lax
from jax.experimental import pallas as pl
from jax.experimental.pallas import tpu as pltpu
from jax.sharding import PartitionSpec as P

BF = jnp.bfloat16
F32 = jnp.float32
PARAMS = pltpu.CompilerParams(vmem_limit_bytes=48 * 1024 * 1024)


def dot(a, b):
    return lax.dot_general(a, b, (((1,), (0,)), ((), ())), preferred_element_type=F32)


def dot_nt(a, b):
    return lax.dot_general(a, b, (((1,), (1,)), ((), ())), preferred_element_type=F32)


def two_part(x):
    high = x.astype(BF)
    return high, (x - high.astype(F32)).astype(BF)


def gather_kernel(asked_ref, table_ref, out_ref, hot_ref):
    groups, width = asked_ref.shape
    rows = table_ref.shape[0]
    columns = jnp.transpose(asked_ref[...].astype(F32))
    lanes = lax.broadcasted_iota(jnp.int32, (width, rows), 1).astype(F32)
    for j in range(groups):
        hot_ref[pl.ds(j * width, width), :] = jnp.where(
            lanes == columns[:, j : j + 1], 1.0, 0.0
        ).astype(BF)
    out_ref[...] = dot(hot_ref[...], table_ref[...]).astype(BF)


def counts_of(selfs, edges_ref, degree_ref, out_ref, height):
    relations, fan, nodes = edges_ref.shape
    slots = lax.broadcasted_iota(jnp.int32, (height, nodes), 0)
    out_ref[:, 0:nodes] = jnp.where(slots == selfs, 1.0, 0.0).astype(BF)
    for r in range(relations):
        degree = degree_ref[r : r + 1, :]
        total = None
        for f in range(fan):
            edge = jnp.where(degree > f, edges_ref[r, f : f + 1, :], -1)
            hit = jnp.where(slots == edge, 1.0, 0.0)
            total = hit if total is None else total + hit
        out_ref[:, (r + 1) * nodes : (r + 2) * nodes] = total.astype(BF)


def inverse_columns(degree_ref):
    relations, nodes = degree_ref.shape
    inverse = 1.0 / degree_ref[...].astype(F32)
    padded = jnp.concatenate([inverse, jnp.ones((8 - relations, nodes), F32)], axis=0)
    return jnp.transpose(padded)


def prepare_kernel(
    self1_ref,
    edges1_ref,
    degree1_ref,
    self2_ref,
    edges2_ref,
    degree2_ref,
    weights_ref,
    cot_ref,
    m1_ref,
    m2_ref,
    wt_ref,
    back_ref,
    column_ref,
    high_ref,
    low_ref,
):
    counts_of(self1_ref[...], edges1_ref, degree1_ref, m1_ref, m1_ref.shape[0])
    counts_of(self2_ref[...], edges2_ref, degree2_ref, m2_ref, m2_ref.shape[0])
    layers, kinds = weights_ref.shape[0], weights_ref.shape[1]
    for layer in range(layers):
        for r in range(kinds):
            wt_ref[layer, r] = jnp.transpose(weights_ref[layer, r].astype(F32)).astype(BF)
    column_ref[...] = inverse_columns(degree1_ref)
    column2 = inverse_columns(degree2_ref)
    seeds = cot_ref.shape[0]
    cot = cot_ref[...]
    for r in range(kinds):
        part = dot_nt(cot, weights_ref[1, r])
        if r > 0:
            part = part * column2[:, r - 1 : r]
        high, low = two_part(part)
        high_ref[pl.ds(r * seeds, seeds), :] = high
        low_ref[pl.ds(r * seeds, seeds), :] = low
    m2 = m2_ref[...]
    back_ref[...] = jnp.transpose(dot(m2, high_ref[...]) + dot(m2, low_ref[...]))


def main_kernel(
    count_ref,
    core_ref,
    x_ref,
    m1_ref,
    m2_ref,
    wt_ref,
    back_ref,
    degree1_ref,
    degree2_ref,
    cot_ref,
    node_ref,
    grad_ref,
    keep_ref,
    send_ref,
    live_ref,
    agg_ref,
    agg2_ref,
):
    shards = count_ref.shape[1]
    slots, feature = x_ref.shape
    width = slots // shards
    kinds = wt_ref.shape[1]
    nodes = degree1_ref.shape[1]
    seeds = degree2_ref.shape[1]
    position = lax.broadcasted_iota(jnp.int32, (width, feature), 0)
    for k in range(shards):
        rows = x_ref[pl.ds(k * width, width), :].astype(F32)
        live_ref[pl.ds(k * width, width), :] = jnp.where(position < count_ref[0, k], rows, 0.0)
    xt = jnp.transpose(live_ref[...]).astype(BF)
    inverse1 = 1.0 / degree1_ref[...].astype(F32)
    inverse2 = 1.0 / degree2_ref[...].astype(F32)
    pre = None
    for r in range(kinds):
        part = dot(xt, m1_ref[:, r * nodes : (r + 1) * nodes])
        if r > 0:
            part = part * inverse1[r - 1 : r, :]
        part = part.astype(BF)
        agg_ref[:, r * nodes : (r + 1) * nodes] = part
        term = dot(wt_ref[0, r], part)
        pre = term if pre is None else pre + term
    logistic = 1.0 / (1.0 + jnp.exp(-pre))
    hidden = (pre * logistic).astype(BF)
    slope = logistic * (1.0 + pre * (1.0 - logistic))
    grad_pre = jnp.transpose(back_ref[...] * slope).astype(BF)
    out = None
    for r in range(kinds):
        part = dot(hidden, m2_ref[:, r * seeds : (r + 1) * seeds])
        if r > 0:
            part = part * inverse2[r - 1 : r, :]
        part = part.astype(BF)
        agg2_ref[:, r * seeds : (r + 1) * seeds] = part
        term = dot(wt_ref[1, r], part)
        out = term if out is None else out + term
    node_ref[...] = jnp.transpose(out).astype(BF)
    grad_ref[...] = grad_pre

    def bottom(r):
        return dot(agg_ref[:, r * nodes : (r + 1) * nodes], grad_pre)

    def top(r):
        return dot(agg2_ref[:, r * seeds : (r + 1) * seeds], cot_ref[...])

    @pl.when(core_ref[0] == 0)
    def first():
        for r in range(kinds):
            keep_ref[r] = bottom(r)
            send_ref[r] = top(r).astype(BF)

    @pl.when(core_ref[0] != 0)
    def second():
        for r in range(kinds):
            keep_ref[r] = top(r)
            send_ref[r] = bottom(r).astype(BF)


def slots_kernel(count_ref, grad_ref, m1_ref, wt_ref, column_ref, slot_ref, spread_ref, live_ref):
    shards = count_ref.shape[1]
    slots, feature = slot_ref.shape
    width = slots // shards
    kinds = wt_ref.shape[1]
    nodes = grad_ref.shape[0]
    position = lax.broadcasted_iota(jnp.int32, (width, feature), 0)
    grad_pre = grad_ref[...]
    for r in range(kinds):
        part = dot(grad_pre, wt_ref[0, r])
        if r > 0:
            part = part * column_ref[:, r - 1 : r]
        spread_ref[pl.ds(r * nodes, nodes), :] = part.astype(BF)
    live_ref[...] = dot(m1_ref[...], spread_ref[...])
    for k in range(shards):
        rows = live_ref[pl.ds(k * width, width), :]
        slot_ref[pl.ds(k * width, width), :] = jnp.where(
            position < count_ref[0, k], rows, 0.0
        ).astype(BF)


def scatter_kernel(asked_ref, grads_ref, out_ref):
    groups, share, feature = out_ref.shape
    rows = groups * share
    index = lax.broadcasted_iota(jnp.int32, (rows, asked_ref.shape[1]), 0)
    hot = jnp.where(index == asked_ref[...], 1.0, 0.0).astype(BF)
    dense = dot(hot, grads_ref[...])
    out_ref[...] = dense.reshape(groups, share, feature).astype(BF)


def whole(n):
    return [pl.BlockSpec(memory_space=pltpu.VMEM)] * n


def shaped(shape, kind):
    return jax.ShapeDtypeStruct(shape, kind)


def body(
    table,
    weights,
    fetch_rows,
    fetch_count,
    first_self,
    first_edges,
    first_degree,
    second_self,
    second_edges,
    second_degree,
    cotangent,
):
    wanted = fetch_rows[0, 0]
    shards, width = wanted.shape
    rows, feature = table.shape
    slots = shards * width
    kinds = weights.shape[1]
    nodes = first_self.shape[2]
    seeds = second_self.shape[2]
    groups = lax.axis_size("dp")
    chips = groups // 2
    core = lax.axis_index("dp") % 2
    swap = [(i, i ^ 1) for i in range(groups)]
    both = ("dp", "table")
    down = 8
    across = shards // down

    def device(z, c, y, x):
        return ((z * 2 + c) * down + y) * across + x

    planes = [
        [device(z, 0, y, x) for y in range(down) for x in range(across)] for z in range(chips)
    ] + [[device(z, 1, y, x) for z in range(chips) for x in range(across)] for y in range(down)]

    def exchange(stride):
        pairs = []
        for z in range(chips):
            for y in range(down):
                for x in range(across):
                    pairs.append((device(z, 0, y, x), device(z ^ stride, 0, y, x)))
                    pairs.append((device(z, 1, y, x), device(z, 1, y ^ stride, x)))
        return pairs

    smem = pl.BlockSpec(memory_space=pltpu.SMEM)

    asked = lax.all_to_all(wanted, "table", split_axis=0, concat_axis=0, tiled=True)

    degree1 = first_degree[0, 0]
    degree2 = second_degree[0, 0]
    cot = cotangent[0, 0]
    m1, m2, wt, back, column = pl.pallas_call(
        prepare_kernel,
        out_shape=(
            shaped((slots, kinds * nodes), BF),
            shaped((nodes, kinds * seeds), BF),
            shaped(weights.shape, BF),
            shaped((feature, nodes), F32),
            shaped((nodes, 8), F32),
        ),
        in_specs=whole(8),
        out_specs=tuple(whole(5)),
        scratch_shapes=[
            pltpu.VMEM((kinds * seeds, feature), BF),
            pltpu.VMEM((kinds * seeds, feature), BF),
        ],
        compiler_params=PARAMS,
        name="prepare",
    )(
        first_self[0],
        jnp.swapaxes(first_edges[0, 0], 1, 2),
        degree1,
        second_self[0],
        jnp.swapaxes(second_edges[0, 0], 1, 2),
        degree2,
        weights,
        cot,
    )

    found = pl.pallas_call(
        gather_kernel,
        out_shape=shaped((slots, feature), BF),
        in_specs=whole(2),
        out_specs=whole(1)[0],
        scratch_shapes=[pltpu.VMEM((slots, rows), BF)],
        compiler_params=PARAMS,
        name="gather",
    )(asked, table)
    inputs = lax.all_to_all(found, "table", split_axis=0, concat_axis=0, tiled=True)

    node_out, grad_pre, keep, send = pl.pallas_call(
        main_kernel,
        out_shape=(
            shaped((seeds, feature), BF),
            shaped((nodes, feature), BF),
            shaped((kinds, feature, feature), F32),
            shaped((kinds, feature, feature), BF),
        ),
        in_specs=[smem, smem] + whole(8),
        out_specs=tuple(whole(4)),
        scratch_shapes=[
            pltpu.VMEM((slots, feature), F32),
            pltpu.VMEM((feature, kinds * nodes), BF),
            pltpu.VMEM((feature, kinds * seeds), BF),
        ],
        compiler_params=PARAMS,
        name="step",
    )(
        fetch_count[0],
        core.reshape(1),
        inputs,
        m1,
        m2,
        wt,
        back,
        degree1,
        degree2,
        cot,
    )
    other = lax.ppermute(send, "dp", swap)
    slot_grads = pl.pallas_call(
        slots_kernel,
        out_shape=shaped((slots, feature), BF),
        in_specs=[smem] + whole(4),
        out_specs=whole(1)[0],
        scratch_shapes=[
            pltpu.VMEM((kinds * nodes, feature), BF),
            pltpu.VMEM((slots, feature), F32),
        ],
        compiler_params=PARAMS,
        name="slots",
    )(fetch_count[0], grad_pre, m1, wt, column)

    half = (keep + other.astype(F32)).astype(BF).reshape(-1, feature)
    scattered = lax.all_to_all(
        half, both, split_axis=0, concat_axis=0, tiled=True, axis_index_groups=planes
    )
    slot_grads, scattered = lax.optimization_barrier((slot_grads, scattered))
    returned = lax.all_to_all(slot_grads, "table", split_axis=0, concat_axis=0, tiled=True)
    total = jnp.sum(scattered.reshape(shards, -1, feature).astype(F32), axis=0)
    for stride in (1, 2, 4):
        total = total + lax.ppermute(total, both, exchange(stride))
    batch = seeds * groups * shards
    mean = (total / jnp.sqrt(jnp.float32(batch))).astype(BF)

    share = rows // groups
    dense = pl.pallas_call(
        scatter_kernel,
        out_shape=shaped((groups, share, feature), BF),
        in_specs=whole(2),
        out_specs=whole(1)[0],
        compiler_params=PARAMS,
        name="scatter",
    )(asked.reshape(1, slots), returned)
    mine_half = lax.all_to_all(
        jnp.broadcast_to(mean[None], (shards,) + mean.shape).reshape(-1, feature),
        both,
        split_axis=0,
        concat_axis=0,
        tiled=True,
        axis_index_groups=planes,
    ).reshape(kinds, feature, feature)
    dense, mine_half = lax.optimization_barrier((dense, mine_half))
    crossed = lax.all_to_all(dense, "dp", split_axis=0, concat_axis=0, tiled=True)
    table_part = jnp.sum(crossed.astype(F32), axis=0)
    other_half = lax.ppermute(mine_half, "dp", swap)
    weight_grad = jnp.stack(
        [
            jnp.where(core == 0, mine_half, other_half),
            jnp.where(core == 0, other_half, mine_half),
        ]
    )
    return (node_out[None, None], weight_grad, table_part[None])


def solution(mesh):
    return jax.shard_map(
        body,
        mesh=mesh,
        in_specs=(
            P("table", None),
            P(),
            P("dp", "table", None, None),
            P("dp", "table", None),
            P("dp", "table", None),
            P("dp", "table", None, None, None),
            P("dp", "table", None, None),
            P("dp", "table", None),
            P("dp", "table", None, None, None),
            P("dp", "table", None, None),
            P("dp", "table", None, None),
        ),
        out_specs=(P("dp", "table", None, None), P(), P("table", "dp", None)),
        check_vma=False,
    )
```

```python
import jax
import jax.numpy as jnp
from jax import lax
from jax.experimental import pallas as pl
from jax.experimental.pallas import tpu as pltpu
from jax.sharding import PartitionSpec as P

BF = jnp.bfloat16
F32 = jnp.float32
PARAMS = pltpu.CompilerParams(vmem_limit_bytes=48 * 1024 * 1024)


def dot(a, b):
    return lax.dot_general(a, b, (((1,), (0,)), ((), ())), preferred_element_type=F32)


def dot_nt(a, b):
    return lax.dot_general(a, b, (((1,), (1,)), ((), ())), preferred_element_type=F32)


def two_part(x):
    high = x.astype(BF)
    return high, (x - high.astype(F32)).astype(BF)


def gather_kernel(asked_ref, table_ref, out_ref, hot_ref):
    groups, width = asked_ref.shape
    rows = table_ref.shape[0]
    columns = jnp.transpose(asked_ref[...].astype(F32))
    lanes = lax.broadcasted_iota(jnp.int32, (width, rows), 1).astype(F32)
    for j in range(groups):
        hot_ref[pl.ds(j * width, width), :] = jnp.where(
            lanes == columns[:, j : j + 1], 1.0, 0.0
        ).astype(BF)
    out_ref[...] = dot(hot_ref[...], table_ref[...]).astype(BF)


def counts_of(selfs, edges_ref, degree_ref, out_ref, height):
    relations, fan, nodes = edges_ref.shape
    slots = lax.broadcasted_iota(jnp.int32, (height, nodes), 0)
    out_ref[:, 0:nodes] = jnp.where(slots == selfs, 1.0, 0.0).astype(BF)
    for r in range(relations):
        degree = degree_ref[r : r + 1, :]
        total = None
        for f in range(fan):
            edge = jnp.where(degree > f, edges_ref[r, f : f + 1, :], -1)
            hit = jnp.where(slots == edge, 1.0, 0.0)
            total = hit if total is None else total + hit
        out_ref[:, (r + 1) * nodes : (r + 2) * nodes] = total.astype(BF)


def inverse_columns(degree_ref):
    relations, nodes = degree_ref.shape
    inverse = 1.0 / degree_ref[...].astype(F32)
    padded = jnp.concatenate([inverse, jnp.ones((8 - relations, nodes), F32)], axis=0)
    return jnp.transpose(padded)


def prepare_kernel(
    self1_ref,
    edges1_ref,
    degree1_ref,
    self2_ref,
    edges2_ref,
    degree2_ref,
    weights_ref,
    cot_ref,
    m1_ref,
    m2_ref,
    wt_ref,
    back_ref,
    column_ref,
    high_ref,
    low_ref,
):
    counts_of(self1_ref[...], edges1_ref, degree1_ref, m1_ref, m1_ref.shape[0])
    counts_of(self2_ref[...], edges2_ref, degree2_ref, m2_ref, m2_ref.shape[0])
    layers, kinds = weights_ref.shape[0], weights_ref.shape[1]
    for layer in range(layers):
        for r in range(kinds):
            wt_ref[layer, r] = jnp.transpose(weights_ref[layer, r].astype(F32)).astype(BF)
    column_ref[...] = inverse_columns(degree1_ref)
    column2 = inverse_columns(degree2_ref)
    seeds = cot_ref.shape[0]
    cot = cot_ref[...]
    for r in range(kinds):
        part = dot_nt(cot, weights_ref[1, r])
        if r > 0:
            part = part * column2[:, r - 1 : r]
        high, low = two_part(part)
        high_ref[pl.ds(r * seeds, seeds), :] = high
        low_ref[pl.ds(r * seeds, seeds), :] = low
    m2 = m2_ref[...]
    back_ref[...] = jnp.transpose(dot(m2, high_ref[...]) + dot(m2, low_ref[...]))


def main_kernel(
    count_ref,
    core_ref,
    x_ref,
    m1_ref,
    m2_ref,
    wt_ref,
    back_ref,
    degree1_ref,
    degree2_ref,
    cot_ref,
    node_ref,
    grad_ref,
    keep_ref,
    send_ref,
    live_ref,
    agg_ref,
    agg2_ref,
):
    shards = count_ref.shape[1]
    slots, feature = x_ref.shape
    width = slots // shards
    kinds = wt_ref.shape[1]
    nodes = degree1_ref.shape[1]
    seeds = degree2_ref.shape[1]
    position = lax.broadcasted_iota(jnp.int32, (width, feature), 0)
    for k in range(shards):
        rows = x_ref[pl.ds(k * width, width), :].astype(F32)
        live_ref[pl.ds(k * width, width), :] = jnp.where(position < count_ref[0, k], rows, 0.0)
    xt = jnp.transpose(live_ref[...]).astype(BF)
    inverse1 = 1.0 / degree1_ref[...].astype(F32)
    inverse2 = 1.0 / degree2_ref[...].astype(F32)
    pre = None
    for r in range(kinds):
        part = dot(xt, m1_ref[:, r * nodes : (r + 1) * nodes])
        if r > 0:
            part = part * inverse1[r - 1 : r, :]
        part = part.astype(BF)
        agg_ref[:, r * nodes : (r + 1) * nodes] = part
        term = dot(wt_ref[0, r], part)
        pre = term if pre is None else pre + term
    logistic = 1.0 / (1.0 + jnp.exp(-pre))
    hidden = (pre * logistic).astype(BF)
    slope = logistic * (1.0 + pre * (1.0 - logistic))
    grad_pre = jnp.transpose(back_ref[...] * slope).astype(BF)
    out = None
    for r in range(kinds):
        part = dot(hidden, m2_ref[:, r * seeds : (r + 1) * seeds])
        if r > 0:
            part = part * inverse2[r - 1 : r, :]
        part = part.astype(BF)
        agg2_ref[:, r * seeds : (r + 1) * seeds] = part
        term = dot(wt_ref[1, r], part)
        out = term if out is None else out + term
    node_ref[...] = jnp.transpose(out).astype(BF)
    grad_ref[...] = grad_pre

    def bottom(r):
        return dot(agg_ref[:, r * nodes : (r + 1) * nodes], grad_pre)

    def top(r):
        return dot(agg2_ref[:, r * seeds : (r + 1) * seeds], cot_ref[...])

    @pl.when(core_ref[0] == 0)
    def first():
        for r in range(kinds):
            keep_ref[r] = bottom(r)
            send_ref[r] = top(r).astype(BF)

    @pl.when(core_ref[0] != 0)
    def second():
        for r in range(kinds):
            keep_ref[r] = top(r)
            send_ref[r] = bottom(r).astype(BF)


def slots_kernel(count_ref, grad_ref, m1_ref, wt_ref, column_ref, slot_ref, spread_ref, live_ref):
    shards = count_ref.shape[1]
    slots, feature = slot_ref.shape
    width = slots // shards
    kinds = wt_ref.shape[1]
    nodes = grad_ref.shape[0]
    position = lax.broadcasted_iota(jnp.int32, (width, feature), 0)
    grad_pre = grad_ref[...]
    for r in range(kinds):
        part = dot(grad_pre, wt_ref[0, r])
        if r > 0:
            part = part * column_ref[:, r - 1 : r]
        spread_ref[pl.ds(r * nodes, nodes), :] = part.astype(BF)
    live_ref[...] = dot(m1_ref[...], spread_ref[...])
    for k in range(shards):
        rows = live_ref[pl.ds(k * width, width), :]
        slot_ref[pl.ds(k * width, width), :] = jnp.where(
            position < count_ref[0, k], rows, 0.0
        ).astype(BF)


def scatter_kernel(asked_ref, grads_ref, out_ref):
    index = lax.broadcasted_iota(jnp.int32, (out_ref.shape[0], asked_ref.shape[1]), 0)
    hot = jnp.where(index == asked_ref[...], 1.0, 0.0).astype(BF)
    out_ref[...] = dot(hot, grads_ref[...])


def whole(n):
    return [pl.BlockSpec(memory_space=pltpu.VMEM)] * n


def shaped(shape, kind):
    return jax.ShapeDtypeStruct(shape, kind)


def body(
    table,
    weights,
    fetch_rows,
    fetch_count,
    first_self,
    first_edges,
    first_degree,
    second_self,
    second_edges,
    second_degree,
    cotangent,
):
    wanted = fetch_rows[0, 0]
    shards, width = wanted.shape
    rows, feature = table.shape
    slots = shards * width
    kinds = weights.shape[1]
    nodes = first_self.shape[2]
    seeds = second_self.shape[2]
    groups = lax.axis_size("dp")
    chips = groups // 2
    core = lax.axis_index("dp") % 2
    swap = [(i, i ^ 1) for i in range(groups)]
    both = ("dp", "table")
    down = 8
    across = shards // down

    def device(z, c, y, x):
        return ((z * 2 + c) * down + y) * across + x

    planes = [
        [device(z, 0, y, x) for y in range(down) for x in range(across)] for z in range(chips)
    ] + [[device(z, 1, y, x) for z in range(chips) for x in range(across)] for y in range(down)]

    lines = [
        [device(z, 0, y, x) for z in range(chips)] for y in range(down) for x in range(across)
    ] + [[device(z, 1, y, x) for y in range(down)] for z in range(chips) for x in range(across)]
    smem = pl.BlockSpec(memory_space=pltpu.SMEM)

    asked = lax.all_to_all(wanted, "table", split_axis=0, concat_axis=0, tiled=True)

    degree1 = first_degree[0, 0]
    degree2 = second_degree[0, 0]
    cot = cotangent[0, 0]
    m1, m2, wt, back, column = pl.pallas_call(
        prepare_kernel,
        out_shape=(
            shaped((slots, kinds * nodes), BF),
            shaped((nodes, kinds * seeds), BF),
            shaped(weights.shape, BF),
            shaped((feature, nodes), F32),
            shaped((nodes, 8), F32),
        ),
        in_specs=whole(8),
        out_specs=tuple(whole(5)),
        scratch_shapes=[
            pltpu.VMEM((kinds * seeds, feature), BF),
            pltpu.VMEM((kinds * seeds, feature), BF),
        ],
        compiler_params=PARAMS,
        name="prepare",
    )(
        first_self[0],
        jnp.swapaxes(first_edges[0, 0], 1, 2),
        degree1,
        second_self[0],
        jnp.swapaxes(second_edges[0, 0], 1, 2),
        degree2,
        weights,
        cot,
    )

    found = pl.pallas_call(
        gather_kernel,
        out_shape=shaped((slots, feature), BF),
        in_specs=whole(2),
        out_specs=whole(1)[0],
        scratch_shapes=[pltpu.VMEM((slots, rows), BF)],
        compiler_params=PARAMS,
        name="gather",
    )(asked, table)
    inputs = lax.all_to_all(found, "table", split_axis=0, concat_axis=0, tiled=True)

    node_out, grad_pre, keep, send = pl.pallas_call(
        main_kernel,
        out_shape=(
            shaped((seeds, feature), BF),
            shaped((nodes, feature), BF),
            shaped((kinds, feature, feature), F32),
            shaped((kinds, feature, feature), BF),
        ),
        in_specs=[smem, smem] + whole(8),
        out_specs=tuple(whole(4)),
        scratch_shapes=[
            pltpu.VMEM((slots, feature), F32),
            pltpu.VMEM((feature, kinds * nodes), BF),
            pltpu.VMEM((feature, kinds * seeds), BF),
        ],
        compiler_params=PARAMS,
        name="step",
    )(
        fetch_count[0],
        core.reshape(1),
        inputs,
        m1,
        m2,
        wt,
        back,
        degree1,
        degree2,
        cot,
    )
    other = lax.ppermute(send, "dp", swap)
    slot_grads = pl.pallas_call(
        slots_kernel,
        out_shape=shaped((slots, feature), BF),
        in_specs=[smem] + whole(4),
        out_specs=whole(1)[0],
        scratch_shapes=[
            pltpu.VMEM((kinds * nodes, feature), BF),
            pltpu.VMEM((slots, feature), F32),
        ],
        compiler_params=PARAMS,
        name="slots",
    )(fetch_count[0], grad_pre, m1, wt, column)

    returned = lax.all_to_all(slot_grads, "table", split_axis=0, concat_axis=0, tiled=True)
    half = (keep + other.astype(F32)).astype(BF).reshape(-1, feature)
    dense = pl.pallas_call(
        scatter_kernel,
        out_shape=shaped((rows, feature), F32),
        in_specs=whole(2),
        out_specs=whole(1)[0],
        compiler_params=PARAMS,
        name="scatter",
    )(asked.reshape(1, slots), returned)
    half, dense = lax.optimization_barrier((half, dense))
    table_part = lax.psum_scatter(dense, "dp", scatter_dimension=0, tiled=True)

    def reduce_weights(half):
        scattered = lax.all_to_all(
            half, both, split_axis=0, concat_axis=0, tiled=True, axis_index_groups=planes
        )
        partial = jnp.sum(scattered.reshape(shards, -1, feature).astype(F32), axis=0).astype(BF)
        crossed = lax.all_to_all(
            jnp.broadcast_to(partial[None], (chips,) + partial.shape).reshape(-1, feature),
            both,
            split_axis=0,
            concat_axis=0,
            tiled=True,
            axis_index_groups=lines,
        )
        total = jnp.sum(crossed.reshape(chips, -1, feature).astype(F32), axis=0)
        batch = seeds * groups * shards
        mean = (total / jnp.sqrt(jnp.float32(batch))).astype(BF)
        mine_half = lax.all_to_all(
            jnp.broadcast_to(mean[None], (shards,) + mean.shape).reshape(-1, feature),
            both,
            split_axis=0,
            concat_axis=0,
            tiled=True,
            axis_index_groups=planes,
        ).reshape(kinds, feature, feature)
        other_half = lax.ppermute(mine_half, "dp", swap)
        return jnp.stack(
            [
                jnp.where(core == 0, mine_half, other_half),
                jnp.where(core == 0, other_half, mine_half),
            ]
        )

    weight_grad = lax.cond(
        fetch_count[0, 0, 0] >= 0,
        reduce_weights,
        lambda half: jnp.zeros((2, kinds, feature, feature), BF),
        half,
    )
    return (node_out[None, None], weight_grad, table_part[None])


def solution(mesh):
    return jax.shard_map(
        body,
        mesh=mesh,
        in_specs=(
            P("table", None),
            P(),
            P("dp", "table", None, None),
            P("dp", "table", None),
            P("dp", "table", None),
            P("dp", "table", None, None, None),
            P("dp", "table", None, None),
            P("dp", "table", None),
            P("dp", "table", None, None, None),
            P("dp", "table", None, None),
            P("dp", "table", None, None),
        ),
        out_specs=(P("dp", "table", None, None), P(), P("table", "dp", None)),
        check_vma=False,
    )
```

```python
import jax
import jax.numpy as jnp
from jax import lax
from jax.experimental import pallas as pl
from jax.experimental.pallas import tpu as pltpu
from jax.sharding import PartitionSpec as P

BF = jnp.bfloat16
F32 = jnp.float32
PARAMS = pltpu.CompilerParams(vmem_limit_bytes=48 * 1024 * 1024)


def dot(a, b):
    return lax.dot_general(a, b, (((1,), (0,)), ((), ())), preferred_element_type=F32)


def dot_nt(a, b):
    return lax.dot_general(a, b, (((1,), (1,)), ((), ())), preferred_element_type=F32)


def two_part(x):
    high = x.astype(BF)
    return high, (x - high.astype(F32)).astype(BF)


def gather_kernel(asked_ref, table_ref, out_ref, hot_ref):
    groups, width = asked_ref.shape
    rows = table_ref.shape[0]
    columns = jnp.transpose(asked_ref[...].astype(F32))
    lanes = lax.broadcasted_iota(jnp.int32, (width, rows), 1).astype(F32)
    for j in range(groups):
        hot_ref[pl.ds(j * width, width), :] = jnp.where(
            lanes == columns[:, j : j + 1], 1.0, 0.0
        ).astype(BF)
    out_ref[...] = dot(hot_ref[...], table_ref[...]).astype(BF)


def counts_of(selfs, edges_ref, degree_ref, out_ref, height):
    relations, fan, nodes = edges_ref.shape
    slots = lax.broadcasted_iota(jnp.int32, (height, nodes), 0)
    out_ref[:, 0:nodes] = jnp.where(slots == selfs, 1.0, 0.0).astype(BF)
    for r in range(relations):
        degree = degree_ref[r : r + 1, :]
        total = None
        for f in range(fan):
            edge = jnp.where(degree > f, edges_ref[r, f : f + 1, :], -1)
            hit = jnp.where(slots == edge, 1.0, 0.0)
            total = hit if total is None else total + hit
        out_ref[:, (r + 1) * nodes : (r + 2) * nodes] = total.astype(BF)


def inverse_columns(degree_ref):
    relations, nodes = degree_ref.shape
    inverse = 1.0 / degree_ref[...].astype(F32)
    padded = jnp.concatenate([inverse, jnp.ones((8 - relations, nodes), F32)], axis=0)
    return jnp.transpose(padded)


def prepare_kernel(
    self1_ref,
    edges1_ref,
    degree1_ref,
    self2_ref,
    edges2_ref,
    degree2_ref,
    weights_ref,
    cot_ref,
    m1_ref,
    m2_ref,
    wt_ref,
    back_ref,
    column_ref,
    high_ref,
    low_ref,
):
    counts_of(self1_ref[...], edges1_ref, degree1_ref, m1_ref, m1_ref.shape[0])
    counts_of(self2_ref[...], edges2_ref, degree2_ref, m2_ref, m2_ref.shape[0])
    layers, kinds = weights_ref.shape[0], weights_ref.shape[1]
    for layer in range(layers):
        for r in range(kinds):
            wt_ref[layer, r] = jnp.transpose(weights_ref[layer, r].astype(F32)).astype(BF)
    column_ref[...] = inverse_columns(degree1_ref)
    column2 = inverse_columns(degree2_ref)
    seeds = cot_ref.shape[0]
    cot = cot_ref[...]
    for r in range(kinds):
        part = dot_nt(cot, weights_ref[1, r])
        if r > 0:
            part = part * column2[:, r - 1 : r]
        high, low = two_part(part)
        high_ref[pl.ds(r * seeds, seeds), :] = high
        low_ref[pl.ds(r * seeds, seeds), :] = low
    m2 = m2_ref[...]
    back_ref[...] = jnp.transpose(dot(m2, high_ref[...]) + dot(m2, low_ref[...]))


def main_kernel(
    count_ref,
    core_ref,
    x_ref,
    m1_ref,
    m2_ref,
    wt_ref,
    back_ref,
    degree1_ref,
    degree2_ref,
    cot_ref,
    node_ref,
    grad_ref,
    keep_ref,
    send_ref,
    live_ref,
    agg_ref,
    agg2_ref,
):
    shards = count_ref.shape[1]
    slots, feature = x_ref.shape
    width = slots // shards
    kinds = wt_ref.shape[1]
    nodes = degree1_ref.shape[1]
    seeds = degree2_ref.shape[1]
    position = lax.broadcasted_iota(jnp.int32, (width, feature), 0)
    for k in range(shards):
        rows = x_ref[pl.ds(k * width, width), :].astype(F32)
        live_ref[pl.ds(k * width, width), :] = jnp.where(position < count_ref[0, k], rows, 0.0)
    xt = jnp.transpose(live_ref[...]).astype(BF)
    inverse1 = 1.0 / degree1_ref[...].astype(F32)
    inverse2 = 1.0 / degree2_ref[...].astype(F32)
    pre = None
    for r in range(kinds):
        part = dot(xt, m1_ref[:, r * nodes : (r + 1) * nodes])
        if r > 0:
            part = part * inverse1[r - 1 : r, :]
        part = part.astype(BF)
        agg_ref[:, r * nodes : (r + 1) * nodes] = part
        term = dot(wt_ref[0, r], part)
        pre = term if pre is None else pre + term
    logistic = 1.0 / (1.0 + jnp.exp(-pre))
    hidden = (pre * logistic).astype(BF)
    slope = logistic * (1.0 + pre * (1.0 - logistic))
    grad_pre = jnp.transpose(back_ref[...] * slope).astype(BF)
    out = None
    for r in range(kinds):
        part = dot(hidden, m2_ref[:, r * seeds : (r + 1) * seeds])
        if r > 0:
            part = part * inverse2[r - 1 : r, :]
        part = part.astype(BF)
        agg2_ref[:, r * seeds : (r + 1) * seeds] = part
        term = dot(wt_ref[1, r], part)
        out = term if out is None else out + term
    node_ref[...] = jnp.transpose(out).astype(BF)
    grad_ref[...] = grad_pre

    def bottom(r):
        return dot(agg_ref[:, r * nodes : (r + 1) * nodes], grad_pre)

    def top(r):
        return dot(agg2_ref[:, r * seeds : (r + 1) * seeds], cot_ref[...])

    @pl.when(core_ref[0] == 0)
    def first():
        for r in range(kinds):
            keep_ref[r] = bottom(r)
            send_ref[r] = top(r).astype(BF)

    @pl.when(core_ref[0] != 0)
    def second():
        for r in range(kinds):
            keep_ref[r] = top(r)
            send_ref[r] = bottom(r).astype(BF)


def slots_kernel(count_ref, grad_ref, m1_ref, wt_ref, column_ref, slot_ref, spread_ref, live_ref):
    shards = count_ref.shape[1]
    slots, feature = slot_ref.shape
    width = slots // shards
    kinds = wt_ref.shape[1]
    nodes = grad_ref.shape[0]
    position = lax.broadcasted_iota(jnp.int32, (width, feature), 0)
    grad_pre = grad_ref[...]
    for r in range(kinds):
        part = dot(grad_pre, wt_ref[0, r])
        if r > 0:
            part = part * column_ref[:, r - 1 : r]
        spread_ref[pl.ds(r * nodes, nodes), :] = part.astype(BF)
    live_ref[...] = dot(m1_ref[...], spread_ref[...])
    for k in range(shards):
        rows = live_ref[pl.ds(k * width, width), :]
        slot_ref[pl.ds(k * width, width), :] = jnp.where(
            position < count_ref[0, k], rows, 0.0
        ).astype(BF)


def scatter_kernel(me_ref, asked_ref, grads_ref, keep_ref, give_ref, hot_ref):
    blocks = 16
    rows, slots = hot_ref.shape
    share = rows // blocks
    half = rows // 2
    asked = asked_ref[...]
    within = lax.broadcasted_iota(jnp.int32, (share, slots), 0)
    for b in range(blocks):
        flip = sum(((b >> n) & 1) << (3 - n) for n in range(4))
        index = within + (me_ref[0] ^ flip) * share
        hot_ref[pl.ds(b * share, share), :] = jnp.where(index == asked, 1.0, 0.0).astype(BF)
    grads = grads_ref[...]
    give_ref[...] = dot(hot_ref[half:, :], grads)
    keep_ref[...] = dot(hot_ref[:half, :], grads)


def whole(n):
    return [pl.BlockSpec(memory_space=pltpu.VMEM)] * n


def shaped(shape, kind):
    return jax.ShapeDtypeStruct(shape, kind)


def body(
    table,
    weights,
    fetch_rows,
    fetch_count,
    first_self,
    first_edges,
    first_degree,
    second_self,
    second_edges,
    second_degree,
    cotangent,
):
    wanted = fetch_rows[0, 0]
    shards, width = wanted.shape
    rows, feature = table.shape
    slots = shards * width
    kinds = weights.shape[1]
    nodes = first_self.shape[2]
    seeds = second_self.shape[2]
    groups = lax.axis_size("dp")
    chips = groups // 2
    core = lax.axis_index("dp") % 2
    swap = [(i, i ^ 1) for i in range(groups)]
    both = ("dp", "table")
    down = 8
    across = shards // down

    def device(z, c, y, x):
        return ((z * 2 + c) * down + y) * across + x

    planes = [
        [device(z, 0, y, x) for y in range(down) for x in range(across)] for z in range(chips)
    ] + [[device(z, 1, y, x) for z in range(chips) for x in range(across)] for y in range(down)]

    lines = [
        [device(z, 0, y, x) for z in range(chips)] for y in range(down) for x in range(across)
    ] + [[device(z, 1, y, x) for y in range(down)] for z in range(chips) for x in range(across)]
    smem = pl.BlockSpec(memory_space=pltpu.SMEM)

    asked = lax.all_to_all(wanted, "table", split_axis=0, concat_axis=0, tiled=True)

    degree1 = first_degree[0, 0]
    degree2 = second_degree[0, 0]
    cot = cotangent[0, 0]
    m1, m2, wt, back, column = pl.pallas_call(
        prepare_kernel,
        out_shape=(
            shaped((slots, kinds * nodes), BF),
            shaped((nodes, kinds * seeds), BF),
            shaped(weights.shape, BF),
            shaped((feature, nodes), F32),
            shaped((nodes, 8), F32),
        ),
        in_specs=whole(8),
        out_specs=tuple(whole(5)),
        scratch_shapes=[
            pltpu.VMEM((kinds * seeds, feature), BF),
            pltpu.VMEM((kinds * seeds, feature), BF),
        ],
        compiler_params=PARAMS,
        name="prepare",
    )(
        first_self[0],
        jnp.swapaxes(first_edges[0, 0], 1, 2),
        degree1,
        second_self[0],
        jnp.swapaxes(second_edges[0, 0], 1, 2),
        degree2,
        weights,
        cot,
    )

    found = pl.pallas_call(
        gather_kernel,
        out_shape=shaped((slots, feature), BF),
        in_specs=whole(2),
        out_specs=whole(1)[0],
        scratch_shapes=[pltpu.VMEM((slots, rows), BF)],
        compiler_params=PARAMS,
        name="gather",
    )(asked, table)
    inputs = lax.all_to_all(found, "table", split_axis=0, concat_axis=0, tiled=True)

    node_out, grad_pre, keep, send = pl.pallas_call(
        main_kernel,
        out_shape=(
            shaped((seeds, feature), BF),
            shaped((nodes, feature), BF),
            shaped((kinds, feature, feature), F32),
            shaped((kinds, feature, feature), BF),
        ),
        in_specs=[smem, smem] + whole(8),
        out_specs=tuple(whole(4)),
        scratch_shapes=[
            pltpu.VMEM((slots, feature), F32),
            pltpu.VMEM((feature, kinds * nodes), BF),
            pltpu.VMEM((feature, kinds * seeds), BF),
        ],
        compiler_params=PARAMS,
        name="step",
    )(
        fetch_count[0],
        core.reshape(1),
        inputs,
        m1,
        m2,
        wt,
        back,
        degree1,
        degree2,
        cot,
    )
    other = lax.ppermute(send, "dp", swap)
    slot_grads = pl.pallas_call(
        slots_kernel,
        out_shape=shaped((slots, feature), BF),
        in_specs=[smem] + whole(4),
        out_specs=whole(1)[0],
        scratch_shapes=[
            pltpu.VMEM((kinds * nodes, feature), BF),
            pltpu.VMEM((slots, feature), F32),
        ],
        compiler_params=PARAMS,
        name="slots",
    )(fetch_count[0], grad_pre, m1, wt, column)

    returned = lax.all_to_all(slot_grads, "table", split_axis=0, concat_axis=0, tiled=True)
    half = (keep + other.astype(F32)).astype(BF).reshape(-1, feature)
    half, returned = lax.optimization_barrier((half, returned))
    share = rows // groups
    keep_rows, give_rows = pl.pallas_call(
        scatter_kernel,
        out_shape=(shaped((rows // 2, feature), F32),) * 2,
        in_specs=[smem] + whole(2),
        out_specs=tuple(whole(2)),
        scratch_shapes=[pltpu.VMEM((rows, slots), BF)],
        compiler_params=PARAMS,
        name="scatter",
    )(lax.axis_index("dp").reshape(1), asked.reshape(1, slots), returned)

    def halve(keep_rows, give_rows, bit):
        got = lax.ppermute(give_rows, "dp", [(i, i ^ bit) for i in range(groups)])
        return keep_rows + got

    scattered = lax.all_to_all(
        half, both, split_axis=0, concat_axis=0, tiled=True, axis_index_groups=planes
    )
    rest = halve(keep_rows, give_rows, 1)
    rest = halve(rest[: rows // 4], rest[rows // 4 :], 2)
    partial = jnp.sum(scattered.reshape(shards, -1, feature).astype(F32), axis=0).astype(BF)
    crossed = lax.all_to_all(
        jnp.broadcast_to(partial[None], (chips,) + partial.shape).reshape(-1, feature),
        both,
        split_axis=0,
        concat_axis=0,
        tiled=True,
        axis_index_groups=lines,
    )
    total = jnp.sum(crossed.reshape(chips, -1, feature).astype(F32), axis=0)
    batch = seeds * groups * shards
    mean = (total / jnp.sqrt(jnp.float32(batch))).astype(BF)
    rest = halve(rest[: rows // 8], rest[rows // 8 :], 4)
    mean, rest = lax.optimization_barrier((mean, rest))
    mine_half = lax.all_to_all(
        jnp.broadcast_to(mean[None], (shards,) + mean.shape).reshape(-1, feature),
        both,
        split_axis=0,
        concat_axis=0,
        tiled=True,
        axis_index_groups=planes,
    ).reshape(kinds, feature, feature)
    table_part = halve(rest[:share], rest[share:], 8)
    mine_half, table_part = lax.optimization_barrier((mine_half, table_part))
    other_half = lax.ppermute(mine_half, "dp", swap)
    weight_grad = jnp.stack(
        [
            jnp.where(core == 0, mine_half, other_half),
            jnp.where(core == 0, other_half, mine_half),
        ]
    )
    return (node_out[None, None], weight_grad, table_part[None])


def solution(mesh):
    return jax.shard_map(
        body,
        mesh=mesh,
        in_specs=(
            P("table", None),
            P(),
            P("dp", "table", None, None),
            P("dp", "table", None),
            P("dp", "table", None),
            P("dp", "table", None, None, None),
            P("dp", "table", None, None),
            P("dp", "table", None),
            P("dp", "table", None, None, None),
            P("dp", "table", None, None),
            P("dp", "table", None, None),
        ),
        out_specs=(P("dp", "table", None, None), P(), P("table", "dp", None)),
        check_vma=False,
    )
```

```python
import jax
import jax.numpy as jnp
from jax import lax
from jax.experimental import pallas as pl
from jax.experimental.pallas import tpu as pltpu
from jax.sharding import PartitionSpec as P

BF = jnp.bfloat16
F32 = jnp.float32
PARAMS = pltpu.CompilerParams(vmem_limit_bytes=20 * 1024 * 1024)


def dot(a, b):
    return lax.dot_general(a, b, (((1,), (0,)), ((), ())), preferred_element_type=F32)


def dot_nt(a, b):
    return lax.dot_general(a, b, (((1,), (1,)), ((), ())), preferred_element_type=F32)


def two_part(x):
    high = x.astype(BF)
    return high, (x - high.astype(F32)).astype(BF)


def gather_kernel(asked_ref, table_ref, out_ref, hot_ref, near_ref, sem):
    copy = pltpu.make_async_copy(table_ref, near_ref, sem)
    copy.start()
    groups, width = asked_ref.shape
    rows = near_ref.shape[0]
    columns = jnp.transpose(asked_ref[...].astype(F32))
    lanes = lax.broadcasted_iota(jnp.int32, (width, rows), 1).astype(F32)
    for j in range(groups):
        hot_ref[pl.ds(j * width, width), :] = jnp.where(
            lanes == columns[:, j : j + 1], 1.0, 0.0
        ).astype(BF)
    copy.wait()
    out_ref[...] = dot(hot_ref[...], near_ref[...]).astype(BF)


def counts_of(selfs, edges_ref, degree_ref, out_ref, height):
    relations, fan, nodes = edges_ref.shape
    slots = lax.broadcasted_iota(jnp.int32, (height, nodes), 0)
    out_ref[:, 0:nodes] = jnp.where(slots == selfs, 1.0, 0.0).astype(BF)
    for r in range(relations):
        degree = degree_ref[r : r + 1, :]
        total = None
        for f in range(fan):
            edge = jnp.where(degree > f, edges_ref[r, f : f + 1, :], -1)
            hit = jnp.where(slots == edge, 1.0, 0.0)
            total = hit if total is None else total + hit
        out_ref[:, (r + 1) * nodes : (r + 2) * nodes] = total.astype(BF)


def inverse_columns(degree_ref):
    relations, nodes = degree_ref.shape
    inverse = 1.0 / degree_ref[...].astype(F32)
    padded = jnp.concatenate([inverse, jnp.ones((8 - relations, nodes), F32)], axis=0)
    return jnp.transpose(padded)


def prepare_kernel(
    self1_ref,
    edges1_ref,
    degree1_ref,
    self2_ref,
    edges2_ref,
    degree2_ref,
    weights_ref,
    cot_ref,
    m1_ref,
    m2_ref,
    wt_ref,
    back_ref,
    column_ref,
    high_ref,
    low_ref,
):
    counts_of(self1_ref[...], edges1_ref, degree1_ref, m1_ref, m1_ref.shape[0])
    counts_of(self2_ref[...], edges2_ref, degree2_ref, m2_ref, m2_ref.shape[0])
    layers, kinds = weights_ref.shape[0], weights_ref.shape[1]
    for layer in range(layers):
        for r in range(kinds):
            wt_ref[layer, r] = jnp.transpose(weights_ref[layer, r].astype(F32)).astype(BF)
    column_ref[...] = inverse_columns(degree1_ref)
    column2 = inverse_columns(degree2_ref)
    seeds = cot_ref.shape[0]
    cot = cot_ref[...]
    for r in range(kinds):
        part = dot_nt(cot, weights_ref[1, r])
        if r > 0:
            part = part * column2[:, r - 1 : r]
        high, low = two_part(part)
        high_ref[pl.ds(r * seeds, seeds), :] = high
        low_ref[pl.ds(r * seeds, seeds), :] = low
    m2 = m2_ref[...]
    back_ref[...] = jnp.transpose(dot(m2, high_ref[...]) + dot(m2, low_ref[...]))


def step_kernel(
    count_ref,
    x_ref,
    m1_ref,
    wt_ref,
    back_ref,
    column_ref,
    degree_ref,
    slot_ref,
    agg_ref,
    hidden_ref,
    grad_ref,
    live_ref,
    spread_ref,
):
    shards = count_ref.shape[1]
    slots, feature = x_ref.shape
    width = slots // shards
    kinds = wt_ref.shape[1]
    nodes = degree_ref.shape[1]
    position = lax.broadcasted_iota(jnp.int32, (width, feature), 0)
    for k in range(shards):
        rows = x_ref[pl.ds(k * width, width), :].astype(F32)
        live_ref[pl.ds(k * width, width), :] = jnp.where(position < count_ref[0, k], rows, 0.0)
    xt = jnp.transpose(live_ref[...]).astype(BF)
    inverse = 1.0 / degree_ref[...].astype(F32)
    pre = None
    for r in range(kinds):
        part = dot(xt, m1_ref[:, r * nodes : (r + 1) * nodes])
        if r > 0:
            part = part * inverse[r - 1 : r, :]
        part = part.astype(BF)
        agg_ref[:, r * nodes : (r + 1) * nodes] = part
        term = dot(wt_ref[0, r], part)
        pre = term if pre is None else pre + term
    logistic = 1.0 / (1.0 + jnp.exp(-pre))
    hidden_ref[...] = (pre * logistic).astype(BF)
    slope = logistic * (1.0 + pre * (1.0 - logistic))
    grad_pre = jnp.transpose(back_ref[...] * slope).astype(BF)
    grad_ref[...] = grad_pre
    for r in range(kinds):
        part = dot(grad_pre, wt_ref[0, r])
        if r > 0:
            part = part * column_ref[:, r - 1 : r]
        spread_ref[pl.ds(r * nodes, nodes), :] = part.astype(BF)
    live_ref[...] = dot(m1_ref[...], spread_ref[...])
    for k in range(shards):
        rows = live_ref[pl.ds(k * width, width), :]
        slot_ref[pl.ds(k * width, width), :] = jnp.where(
            position < count_ref[0, k], rows, 0.0
        ).astype(BF)


def grads_kernel(
    core_ref,
    agg_ref,
    hidden_ref,
    grad_ref,
    m2_ref,
    wt_ref,
    degree_ref,
    cot_ref,
    node_ref,
    keep_ref,
    send_ref,
    send2_ref,
    agg2_ref,
):
    kinds = wt_ref.shape[1]
    nodes = grad_ref.shape[0]
    seeds = cot_ref.shape[0]
    inverse = 1.0 / degree_ref[...].astype(F32)
    hidden = hidden_ref[...]
    out = None
    for r in range(kinds):
        part = dot(hidden, m2_ref[:, r * seeds : (r + 1) * seeds])
        if r > 0:
            part = part * inverse[r - 1 : r, :]
        part = part.astype(BF)
        agg2_ref[:, r * seeds : (r + 1) * seeds] = part
        term = dot(wt_ref[1, r], part)
        out = term if out is None else out + term
    node_ref[...] = jnp.transpose(out).astype(BF)

    def bottom(r):
        return dot(agg_ref[:, r * nodes : (r + 1) * nodes], grad_ref[...])

    def top(r):
        return dot(agg2_ref[:, r * seeds : (r + 1) * seeds], cot_ref[...])

    def send(r, value):
        half = send_ref.shape[0]
        if r < half:
            send_ref[r] = value
        else:
            send2_ref[r - half] = value

    @pl.when(core_ref[0] == 0)
    def first():
        for r in range(kinds):
            keep_ref[r] = bottom(r)
            send(r, top(r).astype(BF))

    @pl.when(core_ref[0] != 0)
    def second():
        for r in range(kinds):
            keep_ref[r] = top(r)
            send(r, bottom(r).astype(BF))


def scatter_kernel(me_ref, asked_ref, grads_ref, keep_ref, give_ref, hot_ref):
    blocks = 16
    rows, slots = hot_ref.shape
    share = rows // blocks
    half = rows // 2
    asked = asked_ref[...]
    within = lax.broadcasted_iota(jnp.int32, (share, slots), 0)
    for b in range(blocks):
        flip = sum(((b >> n) & 1) << (3 - n) for n in range(4))
        index = within + (me_ref[0] ^ flip) * share
        hot_ref[pl.ds(b * share, share), :] = jnp.where(index == asked, 1.0, 0.0).astype(BF)
    grads = grads_ref[...]
    give_ref[...] = dot(hot_ref[half:, :], grads)
    keep_ref[...] = dot(hot_ref[:half, :], grads)


def whole(n):
    return [pl.BlockSpec(memory_space=pltpu.VMEM)] * n


def shaped(shape, kind):
    return jax.ShapeDtypeStruct(shape, kind)


def body(
    table,
    weights,
    fetch_rows,
    fetch_count,
    first_self,
    first_edges,
    first_degree,
    second_self,
    second_edges,
    second_degree,
    cotangent,
):
    wanted = fetch_rows[0, 0]
    shards, width = wanted.shape
    rows, feature = table.shape
    slots = shards * width
    kinds = weights.shape[1]
    nodes = first_self.shape[2]
    seeds = second_self.shape[2]
    groups = lax.axis_size("dp")
    chips = groups // 2
    core = lax.axis_index("dp") % 2
    swap = [(i, i ^ 1) for i in range(groups)]
    both = ("dp", "table")
    down = 8
    across = shards // down

    def device(z, c, y, x):
        return ((z * 2 + c) * down + y) * across + x

    planes = [
        [device(z, 0, y, x) for y in range(down) for x in range(across)] for z in range(chips)
    ] + [[device(z, 1, y, x) for z in range(chips) for x in range(across)] for y in range(down)]

    lines = [
        [device(z, 0, y, x) for z in range(chips)] for y in range(down) for x in range(across)
    ] + [[device(z, 1, y, x) for y in range(down)] for z in range(chips) for x in range(across)]
    smem = pl.BlockSpec(memory_space=pltpu.SMEM)

    asked = lax.all_to_all(wanted, "table", split_axis=0, concat_axis=0, tiled=True)

    degree1 = first_degree[0, 0]
    degree2 = second_degree[0, 0]
    cot = cotangent[0, 0]
    m1, m2, wt, back, column = pl.pallas_call(
        prepare_kernel,
        out_shape=(
            shaped((slots, kinds * nodes), BF),
            shaped((nodes, kinds * seeds), BF),
            shaped(weights.shape, BF),
            shaped((feature, nodes), F32),
            shaped((nodes, 8), F32),
        ),
        in_specs=whole(8),
        out_specs=tuple(whole(5)),
        scratch_shapes=[
            pltpu.VMEM((kinds * seeds, feature), BF),
            pltpu.VMEM((kinds * seeds, feature), BF),
        ],
        compiler_params=PARAMS,
        name="prepare",
    )(
        first_self[0],
        jnp.swapaxes(first_edges[0, 0], 1, 2),
        degree1,
        second_self[0],
        jnp.swapaxes(second_edges[0, 0], 1, 2),
        degree2,
        weights,
        cot,
    )

    found = pl.pallas_call(
        gather_kernel,
        out_shape=shaped((slots, feature), BF),
        in_specs=whole(1) + [pl.BlockSpec(memory_space=pltpu.MemorySpace.HBM)],
        out_specs=whole(1)[0],
        scratch_shapes=[
            pltpu.VMEM((slots, rows), BF),
            pltpu.VMEM((rows, feature), BF),
            pltpu.SemaphoreType.DMA,
        ],
        compiler_params=PARAMS,
        name="gather",
    )(asked, table)
    inputs = lax.all_to_all(found, "table", split_axis=0, concat_axis=0, tiled=True)

    slot_grads, agg, hidden, grad_pre = pl.pallas_call(
        step_kernel,
        out_shape=(
            shaped((slots, feature), BF),
            shaped((feature, kinds * nodes), BF),
            shaped((feature, nodes), BF),
            shaped((nodes, feature), BF),
        ),
        in_specs=[smem] + whole(6),
        out_specs=tuple(whole(4)),
        scratch_shapes=[
            pltpu.VMEM((slots, feature), F32),
            pltpu.VMEM((kinds * nodes, feature), BF),
        ],
        compiler_params=PARAMS,
        name="step",
    )(fetch_count[0], inputs, m1, wt, back, column, degree1)
    returned = lax.all_to_all(slot_grads, "table", split_axis=0, concat_axis=0, tiled=True)

    node_out, keep, send, send2 = pl.pallas_call(
        grads_kernel,
        out_shape=(
            shaped((seeds, feature), BF),
            shaped((kinds, feature, feature), F32),
            shaped((kinds // 2, feature, feature), BF),
            shaped((kinds // 2, feature, feature), BF),
        ),
        in_specs=[smem] + whole(7),
        out_specs=tuple(whole(4)),
        scratch_shapes=[pltpu.VMEM((feature, kinds * seeds), BF)],
        compiler_params=PARAMS,
        name="grads",
    )(core.reshape(1), agg, hidden, grad_pre, m2, wt, degree2, cot)
    other = jnp.concatenate([lax.ppermute(send, "dp", swap), lax.ppermute(send2, "dp", swap)])
    half = (keep + other.astype(F32)).astype(BF).reshape(-1, feature)
    half, returned = lax.optimization_barrier((half, returned))
    share = rows // groups
    keep_rows, give_rows = pl.pallas_call(
        scatter_kernel,
        out_shape=(shaped((rows // 2, feature), F32),) * 2,
        in_specs=[smem] + whole(2),
        out_specs=tuple(whole(2)),
        scratch_shapes=[pltpu.VMEM((rows, slots), BF)],
        compiler_params=PARAMS,
        name="scatter",
    )(lax.axis_index("dp").reshape(1), asked.reshape(1, slots), returned)

    def halve(keep_rows, give_rows, bit):
        got = lax.ppermute(give_rows, "dp", [(i, i ^ bit) for i in range(groups)])
        return keep_rows + got

    scattered = lax.all_to_all(
        half, both, split_axis=0, concat_axis=0, tiled=True, axis_index_groups=planes
    )
    rest = halve(keep_rows, give_rows, 1)
    rest = halve(rest[: rows // 4], rest[rows // 4 :], 2)
    partial = jnp.sum(scattered.reshape(shards, -1, feature).astype(F32), axis=0).astype(BF)
    crossed = lax.all_to_all(
        jnp.broadcast_to(partial[None], (chips,) + partial.shape).reshape(-1, feature),
        both,
        split_axis=0,
        concat_axis=0,
        tiled=True,
        axis_index_groups=lines,
    )
    total = jnp.sum(crossed.reshape(chips, -1, feature).astype(F32), axis=0)
    batch = seeds * groups * shards
    mean = (total / jnp.sqrt(jnp.float32(batch))).astype(BF)
    rest = halve(rest[: rows // 8], rest[rows // 8 :], 4)
    mean, rest = lax.optimization_barrier((mean, rest))
    mine_half = lax.all_to_all(
        jnp.broadcast_to(mean[None], (shards,) + mean.shape).reshape(-1, feature),
        both,
        split_axis=0,
        concat_axis=0,
        tiled=True,
        axis_index_groups=planes,
    ).reshape(kinds, feature, feature)
    table_part = halve(rest[:share], rest[share:], 8)
    mine_half, table_part = lax.optimization_barrier((mine_half, table_part))
    other_half = lax.ppermute(mine_half, "dp", swap)
    weight_grad = jnp.stack(
        [
            jnp.where(core == 0, mine_half, other_half),
            jnp.where(core == 0, other_half, mine_half),
        ]
    )
    return (node_out[None, None], weight_grad, table_part[None])


def solution(mesh):
    return jax.shard_map(
        body,
        mesh=mesh,
        in_specs=(
            P("table", None),
            P(),
            P("dp", "table", None, None),
            P("dp", "table", None),
            P("dp", "table", None),
            P("dp", "table", None, None, None),
            P("dp", "table", None, None),
            P("dp", "table", None),
            P("dp", "table", None, None, None),
            P("dp", "table", None, None),
            P("dp", "table", None, None),
        ),
        out_specs=(P("dp", "table", None, None), P(), P("table", "dp", None)),
        check_vma=False,
    )
```

```python
import jax
import jax.numpy as jnp
from jax import lax
from jax.experimental import pallas as pl
from jax.experimental.pallas import tpu as pltpu
from jax.sharding import PartitionSpec as P

BF = jnp.bfloat16
F32 = jnp.float32
PARAMS = pltpu.CompilerParams(vmem_limit_bytes=58 * 1024 * 1024)
ROOMY = pltpu.CompilerParams(vmem_limit_bytes=52 * 1024 * 1024)


def dot(a, b):
    return lax.dot_general(a, b, (((1,), (0,)), ((), ())), preferred_element_type=F32)


def dot_nt(a, b):
    return lax.dot_general(a, b, (((1,), (1,)), ((), ())), preferred_element_type=F32)


def two_part(x):
    high = x.astype(BF)
    return high, (x - high.astype(F32)).astype(BF)


def gather_kernel(asked_ref, table_ref, out_ref, hot_ref, near_ref, sem):
    copy = pltpu.make_async_copy(table_ref, near_ref, sem)
    copy.start()
    groups, width = asked_ref.shape
    rows = near_ref.shape[0]
    columns = jnp.transpose(asked_ref[...].astype(F32))
    lanes = lax.broadcasted_iota(jnp.int32, (width, rows), 1).astype(F32)
    for j in range(groups):
        hot_ref[pl.ds(j * width, width), :] = jnp.where(
            lanes == columns[:, j : j + 1], 1.0, 0.0
        ).astype(BF)
    copy.wait()
    out_ref[...] = dot(hot_ref[...], near_ref[...]).astype(BF)


def counts_of(selfs, edges_ref, degree_ref, out_ref, height):
    relations, fan, nodes = edges_ref.shape
    slots = lax.broadcasted_iota(jnp.int32, (height, nodes), 0)
    out_ref[:, 0:nodes] = jnp.where(slots == selfs, 1.0, 0.0).astype(BF)
    for r in range(relations):
        degree = degree_ref[:, r * nodes : (r + 1) * nodes]
        total = None
        for f in range(fan):
            edge = jnp.where(degree > f, edges_ref[r, f : f + 1, :], -1)
            hit = jnp.where(slots == edge, 1.0, 0.0)
            total = hit if total is None else total + hit
        out_ref[:, (r + 1) * nodes : (r + 2) * nodes] = total.astype(BF)


def inverse_columns(degree_ref, relations):
    nodes = degree_ref.shape[1] // relations
    inverse = 1.0 / degree_ref[...].astype(F32)
    rows = [inverse[:, r * nodes : (r + 1) * nodes] for r in range(relations)]
    return jnp.transpose(
        jnp.concatenate(rows + [jnp.ones((8 - relations, nodes), F32)], axis=0)
    )


def prepare_kernel(
    self1_ref,
    edges1_ref,
    degree1_ref,
    self2_ref,
    edges2_ref,
    degree2_ref,
    weights_ref,
    cot_ref,
    m1_ref,
    m2_ref,
    wt_ref,
    back_ref,
    column_ref,
    high_ref,
    low_ref,
):
    counts_of(self1_ref[...], edges1_ref, degree1_ref, m1_ref, m1_ref.shape[0])
    counts_of(self2_ref[...], edges2_ref, degree2_ref, m2_ref, m2_ref.shape[0])
    layers, kinds = weights_ref.shape[0], weights_ref.shape[1]
    for layer in range(layers):
        for r in range(kinds):
            wt_ref[layer, r] = jnp.transpose(weights_ref[layer, r].astype(F32)).astype(BF)
    column_ref[...] = inverse_columns(degree1_ref, edges1_ref.shape[0])
    column2 = inverse_columns(degree2_ref, edges2_ref.shape[0])
    seeds = cot_ref.shape[0]
    cot = cot_ref[...]
    for r in range(kinds):
        part = dot_nt(cot, weights_ref[1, r])
        if r > 0:
            part = part * column2[:, r - 1 : r]
        high, low = two_part(part)
        high_ref[pl.ds(r * seeds, seeds), :] = high
        low_ref[pl.ds(r * seeds, seeds), :] = low
    m2 = m2_ref[...]
    back_ref[...] = jnp.transpose(dot(m2, high_ref[...]) + dot(m2, low_ref[...]))


def step_kernel(
    count_ref,
    x_ref,
    m1_far,
    wt_far,
    back_ref,
    column_ref,
    degree_ref,
    slot_ref,
    agg_ref,
    hidden_ref,
    grad_ref,
    live_ref,
    spread_ref,
    m1_ref,
    wt_ref,
    sems,
):
    copies = [
        pltpu.make_async_copy(m1_far, m1_ref, sems.at[0]),
        pltpu.make_async_copy(wt_far.at[pl.ds(0, 1)], wt_ref, sems.at[1]),
    ]
    for copy in copies:
        copy.start()
    shards = count_ref.shape[1]
    slots, feature = x_ref.shape
    width = slots // shards
    kinds = wt_ref.shape[1]
    nodes = grad_ref.shape[0]
    position = lax.broadcasted_iota(jnp.int32, (width, feature), 0)
    for k in range(shards):
        rows = x_ref[pl.ds(k * width, width), :].astype(F32)
        live_ref[pl.ds(k * width, width), :] = jnp.where(position < count_ref[0, k], rows, 0.0)
    xt = jnp.transpose(live_ref[...]).astype(BF)
    inverse = 1.0 / degree_ref[...].astype(F32)
    for copy in copies:
        copy.wait()
    pre = None
    for r in range(kinds):
        part = dot(xt, m1_ref[:, r * nodes : (r + 1) * nodes])
        if r > 0:
            part = part * inverse[:, (r - 1) * nodes : r * nodes]
        part = part.astype(BF)
        agg_ref[:, r * nodes : (r + 1) * nodes] = part
        term = dot(wt_ref[0, r], part)
        pre = term if pre is None else pre + term
    logistic = 1.0 / (1.0 + jnp.exp(-pre))
    hidden_ref[...] = (pre * logistic).astype(BF)
    slope = logistic * (1.0 + pre * (1.0 - logistic))
    grad_pre = jnp.transpose(back_ref[...] * slope).astype(BF)
    grad_ref[...] = grad_pre
    for r in range(kinds):
        part = dot(grad_pre, wt_ref[0, r])
        if r > 0:
            part = part * column_ref[:, r - 1 : r]
        spread_ref[pl.ds(r * nodes, nodes), :] = part.astype(BF)
    live_ref[...] = dot(m1_ref[...], spread_ref[...])
    for k in range(shards):
        rows = live_ref[pl.ds(k * width, width), :]
        slot_ref[pl.ds(k * width, width), :] = jnp.where(
            position < count_ref[0, k], rows, 0.0
        ).astype(BF)


def grads_kernel(
    core_ref,
    agg_ref,
    hidden_ref,
    grad_ref,
    m2_ref,
    wt_ref,
    degree_ref,
    cot_ref,
    node_ref,
    keep_ref,
    send_ref,
    send2_ref,
    agg2_ref,
):
    kinds = wt_ref.shape[1]
    nodes = grad_ref.shape[0]
    seeds = cot_ref.shape[0]
    inverse = 1.0 / degree_ref[...].astype(F32)
    hidden = hidden_ref[...]
    out = None
    for r in range(kinds):
        part = dot(hidden, m2_ref[:, r * seeds : (r + 1) * seeds])
        if r > 0:
            part = part * inverse[:, (r - 1) * seeds : r * seeds]
        part = part.astype(BF)
        agg2_ref[:, r * seeds : (r + 1) * seeds] = part
        term = dot(wt_ref[1, r], part)
        out = term if out is None else out + term
    node_ref[...] = jnp.transpose(out).astype(BF)

    def bottom(r):
        return dot(agg_ref[:, r * nodes : (r + 1) * nodes], grad_ref[...])

    def top(r):
        return dot(agg2_ref[:, r * seeds : (r + 1) * seeds], cot_ref[...])

    def send(r, value):
        half = send_ref.shape[0]
        if r < half:
            send_ref[r] = value
        else:
            send2_ref[r - half] = value

    @pl.when(core_ref[0] == 0)
    def first():
        for r in range(kinds):
            keep_ref[r] = bottom(r)
            send(r, top(r).astype(BF))

    @pl.when(core_ref[0] != 0)
    def second():
        for r in range(kinds):
            keep_ref[r] = top(r)
            send(r, bottom(r).astype(BF))


def scatter_kernel(me_ref, asked_ref, grads_ref, keep_ref, give_ref, hot_ref):
    blocks = 16
    rows, slots = hot_ref.shape
    share = rows // blocks
    half = rows // 2
    asked = asked_ref[...]
    within = lax.broadcasted_iota(jnp.int32, (share, slots), 0)
    for b in range(blocks):
        flip = sum(((b >> n) & 1) << (3 - n) for n in range(4))
        index = within + (me_ref[0] ^ flip) * share
        hot_ref[pl.ds(b * share, share), :] = jnp.where(index == asked, 1.0, 0.0).astype(BF)
    grads = grads_ref[...]
    give_ref[...] = dot(hot_ref[half:, :], grads)
    keep_ref[...] = dot(hot_ref[:half, :], grads)


def whole(n):
    return [pl.BlockSpec(memory_space=pltpu.VMEM)] * n


def shaped(shape, kind):
    return jax.ShapeDtypeStruct(shape, kind)


def body(
    table,
    weights,
    fetch_rows,
    fetch_count,
    first_self,
    first_edges,
    first_degree,
    second_self,
    second_edges,
    second_degree,
    cotangent,
):
    wanted = fetch_rows[0, 0]
    shards, width = wanted.shape
    rows, feature = table.shape
    slots = shards * width
    kinds = weights.shape[1]
    nodes = first_self.shape[2]
    seeds = second_self.shape[2]
    groups = lax.axis_size("dp")
    chips = groups // 2
    core = lax.axis_index("dp") % 2
    swap = [(i, i ^ 1) for i in range(groups)]
    both = ("dp", "table")
    down = 8
    across = shards // down

    def device(z, c, y, x):
        return ((z * 2 + c) * down + y) * across + x

    planes = [
        [device(z, 0, y, x) for y in range(down) for x in range(across)] for z in range(chips)
    ] + [[device(z, 1, y, x) for z in range(chips) for x in range(across)] for y in range(down)]

    lines = [
        [device(z, 0, y, x) for z in range(chips)] for y in range(down) for x in range(across)
    ] + [[device(z, 1, y, x) for y in range(down)] for z in range(chips) for x in range(across)]
    far = pl.BlockSpec(memory_space=pl.ANY)
    smem = pl.BlockSpec(memory_space=pltpu.SMEM)

    asked = lax.all_to_all(wanted, "table", split_axis=0, concat_axis=0, tiled=True)

    degree1 = first_degree.reshape(1, -1)
    degree2 = second_degree.reshape(1, -1)
    cot = cotangent[0, 0]
    m1, m2, wt, back, column = pl.pallas_call(
        prepare_kernel,
        out_shape=(
            shaped((slots, kinds * nodes), BF),
            shaped((nodes, kinds * seeds), BF),
            shaped(weights.shape, BF),
            shaped((feature, nodes), F32),
            shaped((nodes, 8), F32),
        ),
        in_specs=whole(8),
        out_specs=tuple(whole(5)),
        scratch_shapes=[
            pltpu.VMEM((kinds * seeds, feature), BF),
            pltpu.VMEM((kinds * seeds, feature), BF),
        ],
        compiler_params=PARAMS,
        name="prepare",
    )(
        first_self[0],
        jnp.swapaxes(first_edges[0, 0], 1, 2),
        degree1,
        second_self[0],
        jnp.swapaxes(second_edges[0, 0], 1, 2),
        degree2,
        weights,
        cot,
    )

    found = pl.pallas_call(
        gather_kernel,
        out_shape=shaped((slots, feature), BF),
        in_specs=whole(1) + [far],
        out_specs=whole(1)[0],
        scratch_shapes=[
            pltpu.VMEM((slots, rows), BF),
            pltpu.VMEM((rows, feature), BF),
            pltpu.SemaphoreType.DMA,
        ],
        compiler_params=PARAMS,
        name="gather",
    )(asked, table)
    inputs = lax.all_to_all(found, "table", split_axis=0, concat_axis=0, tiled=True)

    slot_grads, agg, hidden, grad_pre = pl.pallas_call(
        step_kernel,
        out_shape=(
            shaped((slots, feature), BF),
            shaped((feature, kinds * nodes), BF),
            shaped((feature, nodes), BF),
            shaped((nodes, feature), BF),
        ),
        in_specs=[smem] + whole(1) + [far] * 2 + whole(3),
        out_specs=tuple(whole(4)),
        scratch_shapes=[
            pltpu.VMEM((slots, feature), F32),
            pltpu.VMEM((kinds * nodes, feature), BF),
            pltpu.VMEM((slots, kinds * nodes), BF),
            pltpu.VMEM((1, kinds, feature, feature), BF),
            pltpu.SemaphoreType.DMA((2,)),
        ],
        compiler_params=PARAMS,
        name="step",
    )(fetch_count[0], inputs, m1, wt, back, column, degree1)
    returned = lax.all_to_all(slot_grads, "table", split_axis=0, concat_axis=0, tiled=True)

    node_out, keep, send, send2 = pl.pallas_call(
        grads_kernel,
        out_shape=(
            shaped((seeds, feature), BF),
            shaped((kinds, feature, feature), F32),
            shaped((kinds // 2, feature, feature), BF),
            shaped((kinds // 2, feature, feature), BF),
        ),
        in_specs=[smem] + whole(7),
        out_specs=tuple(whole(4)),
        scratch_shapes=[pltpu.VMEM((feature, kinds * seeds), BF)],
        compiler_params=PARAMS,
        name="grads",
    )(core.reshape(1), agg, hidden, grad_pre, m2, wt, degree2, cot)
    other = jnp.concatenate([lax.ppermute(send, "dp", swap), lax.ppermute(send2, "dp", swap)])
    half = (keep + other.astype(F32)).astype(BF).reshape(-1, feature)
    half, returned = lax.optimization_barrier((half, returned))
    share = rows // groups
    keep_rows, give_rows = pl.pallas_call(
        scatter_kernel,
        out_shape=(shaped((rows // 2, feature), F32),) * 2,
        in_specs=[smem] + whole(2),
        out_specs=tuple(whole(2)),
        scratch_shapes=[pltpu.VMEM((rows, slots), BF)],
        compiler_params=ROOMY,
        name="scatter",
    )(lax.axis_index("dp").reshape(1), asked.reshape(1, slots), returned)

    def halve(keep_rows, give_rows, bit):
        got = lax.ppermute(give_rows, "dp", [(i, i ^ bit) for i in range(groups)])
        return keep_rows + got

    scattered = lax.all_to_all(
        half, both, split_axis=0, concat_axis=0, tiled=True, axis_index_groups=planes
    )
    rest = halve(keep_rows, give_rows, 1)
    rest = halve(rest[: rows // 4], rest[rows // 4 :], 2)
    partial = jnp.sum(scattered.reshape(shards, -1, feature).astype(F32), axis=0).astype(BF)
    crossed = lax.all_to_all(
        jnp.broadcast_to(partial[None], (chips,) + partial.shape).reshape(-1, feature),
        both,
        split_axis=0,
        concat_axis=0,
        tiled=True,
        axis_index_groups=lines,
    )
    total = jnp.sum(crossed.reshape(chips, -1, feature).astype(F32), axis=0)
    batch = seeds * groups * shards
    mean = (total / jnp.sqrt(jnp.float32(batch))).astype(BF)
    rest = halve(rest[: rows // 8], rest[rows // 8 :], 4)
    mean, rest = lax.optimization_barrier((mean, rest))
    mine_half = lax.all_to_all(
        jnp.broadcast_to(mean[None], (shards,) + mean.shape).reshape(-1, feature),
        both,
        split_axis=0,
        concat_axis=0,
        tiled=True,
        axis_index_groups=planes,
    ).reshape(kinds, feature, feature)
    table_part = halve(rest[:share], rest[share:], 8)
    mine_half, table_part = lax.optimization_barrier((mine_half, table_part))
    other_half = lax.ppermute(mine_half, "dp", swap)
    weight_grad = jnp.stack(
        [
            jnp.where(core == 0, mine_half, other_half),
            jnp.where(core == 0, other_half, mine_half),
        ]
    )
    return (node_out[None, None], weight_grad, table_part[None])


def solution(mesh):
    return jax.shard_map(
        body,
        mesh=mesh,
        in_specs=(
            P("table", None),
            P(),
            P("dp", "table", None, None),
            P("dp", "table", None),
            P("dp", "table", None),
            P("dp", "table", None, None, None),
            P("dp", "table", None, None),
            P("dp", "table", None),
            P("dp", "table", None, None, None),
            P("dp", "table", None, None),
            P("dp", "table", None, None),
        ),
        out_specs=(P("dp", "table", None, None), P(), P("table", "dp", None)),
        check_vma=False,
    )
```

```python
import jax
import jax.numpy as jnp
from jax import lax
from jax.experimental import pallas as pl
from jax.experimental.pallas import tpu as pltpu
from jax.sharding import PartitionSpec as P

BF = jnp.bfloat16
F32 = jnp.float32
PIECES = 4
PARAMS = pltpu.CompilerParams(vmem_limit_bytes=58 * 1024 * 1024)
ROOMY = pltpu.CompilerParams(vmem_limit_bytes=52 * 1024 * 1024)


def dot(a, b):
    return lax.dot_general(a, b, (((1,), (0,)), ((), ())), preferred_element_type=F32)


def dot_nt(a, b):
    return lax.dot_general(a, b, (((1,), (1,)), ((), ())), preferred_element_type=F32)


def two_part(x):
    high = x.astype(BF)
    return high, (x - high.astype(F32)).astype(BF)


def gather_kernel(asked_ref, table_far, out_far, hot_ref, table_ref, out_ref, sems):
    load = pltpu.make_async_copy(table_far, table_ref, sems.at[0])
    load.start()
    groups, width = asked_ref.shape
    slots, rows = hot_ref.shape
    columns = jnp.transpose(asked_ref[...].astype(F32))
    lanes = lax.broadcasted_iota(jnp.int32, (width, rows), 1).astype(F32)
    for j in range(groups):
        hot_ref[pl.ds(j * width, width), :] = jnp.where(
            lanes == columns[:, j : j + 1], 1.0, 0.0
        ).astype(BF)
    load.wait()
    size = slots // PIECES
    stores = []
    for n in range(PIECES):
        part = pl.ds(n * size, size)
        out_ref[part, :] = dot(hot_ref[part, :], table_ref[...]).astype(BF)
        stores.append(pltpu.make_async_copy(out_ref.at[part], out_far.at[part], sems.at[1 + n]))
        stores[n].start()
    for store in stores:
        store.wait()


def counts_of(selfs, edges_ref, degree_ref, out_ref, height):
    relations, fan, nodes = edges_ref.shape
    slots = lax.broadcasted_iota(jnp.int32, (height, nodes), 0)
    out_ref[:, 0:nodes] = jnp.where(slots == selfs, 1.0, 0.0).astype(BF)
    for r in range(relations):
        degree = degree_ref[:, r * nodes : (r + 1) * nodes]
        total = None
        for f in range(fan):
            edge = jnp.where(degree > f, edges_ref[r, f : f + 1, :], -1)
            hit = jnp.where(slots == edge, 1.0, 0.0)
            total = hit if total is None else total + hit
        out_ref[:, (r + 1) * nodes : (r + 2) * nodes] = total.astype(BF)


def inverse_columns(degree_ref, relations):
    nodes = degree_ref.shape[1] // relations
    inverse = 1.0 / degree_ref[...].astype(F32)
    rows = [inverse[:, r * nodes : (r + 1) * nodes] for r in range(relations)]
    return jnp.transpose(
        jnp.concatenate(rows + [jnp.ones((8 - relations, nodes), F32)], axis=0)
    )


def prepare_kernel(
    self1_ref,
    edges1_ref,
    degree1_ref,
    self2_ref,
    edges2_ref,
    degree2_ref,
    weights_ref,
    cot_ref,
    m1_ref,
    m2_ref,
    wt_ref,
    back_ref,
    column_ref,
    high_ref,
    low_ref,
):
    counts_of(self1_ref[...], edges1_ref, degree1_ref, m1_ref, m1_ref.shape[0])
    counts_of(self2_ref[...], edges2_ref, degree2_ref, m2_ref, m2_ref.shape[0])
    layers, kinds = weights_ref.shape[0], weights_ref.shape[1]
    for layer in range(layers):
        for r in range(kinds):
            wt_ref[layer, r] = jnp.transpose(weights_ref[layer, r].astype(F32)).astype(BF)
    column_ref[...] = inverse_columns(degree1_ref, edges1_ref.shape[0])
    column2 = inverse_columns(degree2_ref, edges2_ref.shape[0])
    seeds = cot_ref.shape[0]
    cot = cot_ref[...]
    for r in range(kinds):
        part = dot_nt(cot, weights_ref[1, r])
        if r > 0:
            part = part * column2[:, r - 1 : r]
        high, low = two_part(part)
        high_ref[pl.ds(r * seeds, seeds), :] = high
        low_ref[pl.ds(r * seeds, seeds), :] = low
    m2 = m2_ref[...]
    back_ref[...] = jnp.transpose(dot(m2, high_ref[...]) + dot(m2, low_ref[...]))


def step_kernel(
    count_ref,
    x_far,
    m1_far,
    wt_far,
    back_far,
    column_far,
    degree_far,
    slot_far,
    agg_far,
    hidden_far,
    grad_far,
    x_ref,
    m1_ref,
    wt_ref,
    back_ref,
    column_ref,
    degree_ref,
    slot_ref,
    agg_ref,
    hidden_ref,
    grad_ref,
    xt_ref,
    spread_ref,
    sems,
):
    shards = count_ref.shape[1]
    slots, feature = x_ref.shape
    width = slots // shards
    kinds = wt_ref.shape[1]
    nodes = grad_ref.shape[0]
    size = slots // PIECES
    pieces = [pl.ds(n * size, size) for n in range(PIECES)]
    x_loads = [
        pltpu.make_async_copy(x_far.at[part], x_ref.at[part], sems.at[n])
        for n, part in enumerate(pieces)
    ]
    used = PIECES
    loads = [
        pltpu.make_async_copy(source, target, sems.at[used + n])
        for n, (source, target) in enumerate(
            [
                (m1_far, m1_ref),
                (wt_far.at[pl.ds(0, 1)], wt_ref),
                (degree_far, degree_ref),
                (back_far, back_ref),
                (column_far, column_ref),
            ]
        )
    ]
    used += len(loads)
    for load in x_loads + loads:
        load.start()
    position = lax.broadcasted_iota(jnp.int32, (width, feature), 0)
    per_piece = shards // PIECES
    for n in range(PIECES):
        x_loads[n].wait()
        rows = []
        for k in range(n * per_piece, (n + 1) * per_piece):
            block = x_ref[pl.ds(k * width, width), :].astype(F32)
            rows.append(jnp.where(position < count_ref[0, k], block, 0.0))
        xt_ref[:, pieces[n]] = jnp.transpose(jnp.concatenate(rows, axis=0)).astype(BF)
    for load in loads:
        load.wait()
    xt = xt_ref[...]
    inverse = 1.0 / degree_ref[...].astype(F32)
    pre = None
    for r in range(kinds):
        part = dot(xt, m1_ref[:, r * nodes : (r + 1) * nodes])
        if r > 0:
            part = part * inverse[:, (r - 1) * nodes : r * nodes]
        part = part.astype(BF)
        agg_ref[:, r * nodes : (r + 1) * nodes] = part
        term = dot(wt_ref[0, r], part)
        pre = term if pre is None else pre + term
    stores = [pltpu.make_async_copy(agg_ref, agg_far, sems.at[used])]
    logistic = 1.0 / (1.0 + jnp.exp(-pre))
    hidden_ref[...] = (pre * logistic).astype(BF)
    stores.append(pltpu.make_async_copy(hidden_ref, hidden_far, sems.at[used + 1]))
    slope = logistic * (1.0 + pre * (1.0 - logistic))
    grad_pre = jnp.transpose(back_ref[...] * slope).astype(BF)
    grad_ref[...] = grad_pre
    stores.append(pltpu.make_async_copy(grad_ref, grad_far, sems.at[used + 2]))
    for store in stores:
        store.start()
    used += len(stores)
    for r in range(kinds):
        part = dot(grad_pre, wt_ref[0, r])
        if r > 0:
            part = part * column_ref[:, r - 1 : r]
        spread_ref[pl.ds(r * nodes, nodes), :] = part.astype(BF)
    spread = spread_ref[...]
    for n in range(PIECES):
        grads = dot(m1_ref[pieces[n], :], spread)
        for k in range(n * per_piece, (n + 1) * per_piece):
            first = (k - n * per_piece) * width
            slot_ref[pl.ds(k * width, width), :] = jnp.where(
                position < count_ref[0, k], grads[first : first + width, :], 0.0
            ).astype(BF)
        store = pltpu.make_async_copy(
            slot_ref.at[pieces[n]], slot_far.at[pieces[n]], sems.at[used + n]
        )
        store.start()
        stores.append(store)
    for store in stores:
        store.wait()


def grads_kernel(
    core_ref,
    agg_ref,
    hidden_ref,
    grad_ref,
    m2_ref,
    wt_ref,
    degree_ref,
    cot_ref,
    node_ref,
    keep_ref,
    send_ref,
    send2_ref,
    agg2_ref,
):
    kinds = wt_ref.shape[1]
    nodes = grad_ref.shape[0]
    seeds = cot_ref.shape[0]
    inverse = 1.0 / degree_ref[...].astype(F32)
    hidden = hidden_ref[...]
    out = None
    for r in range(kinds):
        part = dot(hidden, m2_ref[:, r * seeds : (r + 1) * seeds])
        if r > 0:
            part = part * inverse[:, (r - 1) * seeds : r * seeds]
        part = part.astype(BF)
        agg2_ref[:, r * seeds : (r + 1) * seeds] = part
        term = dot(wt_ref[1, r], part)
        out = term if out is None else out + term
    node_ref[...] = jnp.transpose(out).astype(BF)

    def bottom(r):
        return dot(agg_ref[:, r * nodes : (r + 1) * nodes], grad_ref[...])

    def top(r):
        return dot(agg2_ref[:, r * seeds : (r + 1) * seeds], cot_ref[...])

    def send(r, value):
        half = send_ref.shape[0]
        if r < half:
            send_ref[r] = value
        else:
            send2_ref[r - half] = value

    @pl.when(core_ref[0] == 0)
    def first():
        for r in range(kinds):
            keep_ref[r] = bottom(r)
            send(r, top(r).astype(BF))

    @pl.when(core_ref[0] != 0)
    def second():
        for r in range(kinds):
            keep_ref[r] = top(r)
            send(r, bottom(r).astype(BF))


def scatter_kernel(me_ref, asked_ref, grads_ref, keep_ref, give_ref, hot_ref):
    blocks = 16
    rows, slots = hot_ref.shape
    share = rows // blocks
    half = rows // 2
    asked = asked_ref[...]
    within = lax.broadcasted_iota(jnp.int32, (share, slots), 0)
    for b in range(blocks):
        flip = sum(((b >> n) & 1) << (3 - n) for n in range(4))
        index = within + (me_ref[0] ^ flip) * share
        hot_ref[pl.ds(b * share, share), :] = jnp.where(index == asked, 1.0, 0.0).astype(BF)
    grads = grads_ref[...]
    give_ref[...] = dot(hot_ref[half:, :], grads)
    keep_ref[...] = dot(hot_ref[:half, :], grads)


def place_kernel(layer_ref, half_far, out_far, sem):
    copy = pltpu.make_async_copy(half_far, out_far.at[layer_ref[0]], sem)
    copy.start()
    copy.wait()


def place_other_kernel(layer_ref, half_far, rest_far, out_far, sem):
    place_kernel(layer_ref, half_far, out_far, sem)


def whole(n):
    return [pl.BlockSpec(memory_space=pltpu.VMEM)] * n


def shaped(shape, kind):
    return jax.ShapeDtypeStruct(shape, kind)


def body(
    table,
    weights,
    fetch_rows,
    fetch_count,
    first_self,
    first_edges,
    first_degree,
    second_self,
    second_edges,
    second_degree,
    cotangent,
):
    wanted = fetch_rows[0, 0]
    shards, width = wanted.shape
    rows, feature = table.shape
    slots = shards * width
    kinds = weights.shape[1]
    nodes = first_self.shape[2]
    seeds = second_self.shape[2]
    groups = lax.axis_size("dp")
    chips = groups // 2
    core = lax.axis_index("dp") % 2
    swap = [(i, i ^ 1) for i in range(groups)]
    both = ("dp", "table")
    down = 8
    across = shards // down

    def device(z, c, y, x):
        return ((z * 2 + c) * down + y) * across + x

    planes = [
        [device(z, 0, y, x) for y in range(down) for x in range(across)] for z in range(chips)
    ] + [[device(z, 1, y, x) for z in range(chips) for x in range(across)] for y in range(down)]

    lines = [
        [device(z, 0, y, x) for z in range(chips)] for y in range(down) for x in range(across)
    ] + [[device(z, 1, y, x) for y in range(down)] for z in range(chips) for x in range(across)]
    far = pl.BlockSpec(memory_space=pl.ANY)
    smem = pl.BlockSpec(memory_space=pltpu.SMEM)

    asked = lax.all_to_all(wanted, "table", split_axis=0, concat_axis=0, tiled=True)

    degree1 = first_degree.reshape(1, -1)
    degree2 = second_degree.reshape(1, -1)
    cot = cotangent[0, 0]
    m1, m2, wt, back, column = pl.pallas_call(
        prepare_kernel,
        out_shape=(
            shaped((slots, kinds * nodes), BF),
            shaped((nodes, kinds * seeds), BF),
            shaped(weights.shape, BF),
            shaped((feature, nodes), F32),
            shaped((nodes, 8), F32),
        ),
        in_specs=whole(8),
        out_specs=tuple(whole(5)),
        scratch_shapes=[
            pltpu.VMEM((kinds * seeds, feature), BF),
            pltpu.VMEM((kinds * seeds, feature), BF),
        ],
        compiler_params=PARAMS,
        name="prepare",
    )(
        first_self[0],
        jnp.swapaxes(first_edges[0, 0], 1, 2),
        degree1,
        second_self[0],
        jnp.swapaxes(second_edges[0, 0], 1, 2),
        degree2,
        weights,
        cot,
    )

    found = pl.pallas_call(
        gather_kernel,
        out_shape=shaped((slots, feature), BF),
        in_specs=whole(1) + [far],
        out_specs=far,
        scratch_shapes=[
            pltpu.VMEM((slots, rows), BF),
            pltpu.VMEM((rows, feature), BF),
            pltpu.VMEM((slots, feature), BF),
            pltpu.SemaphoreType.DMA((1 + PIECES,)),
        ],
        compiler_params=PARAMS,
        name="gather",
    )(asked, table)
    inputs = lax.all_to_all(found, "table", split_axis=0, concat_axis=0, tiled=True)

    slot_grads, agg, hidden, grad_pre = pl.pallas_call(
        step_kernel,
        out_shape=(
            shaped((slots, feature), BF),
            shaped((feature, kinds * nodes), BF),
            shaped((feature, nodes), BF),
            shaped((nodes, feature), BF),
        ),
        in_specs=[smem] + [far] * 6,
        out_specs=(far,) * 4,
        scratch_shapes=[
            pltpu.VMEM((slots, feature), BF),
            pltpu.VMEM((slots, kinds * nodes), BF),
            pltpu.VMEM((1, kinds, feature, feature), BF),
            pltpu.VMEM((feature, nodes), F32),
            pltpu.VMEM((nodes, 8), F32),
            pltpu.VMEM(degree1.shape, jnp.int32),
            pltpu.VMEM((slots, feature), BF),
            pltpu.VMEM((feature, kinds * nodes), BF),
            pltpu.VMEM((feature, nodes), BF),
            pltpu.VMEM((nodes, feature), BF),
            pltpu.VMEM((feature, slots), BF),
            pltpu.VMEM((kinds * nodes, feature), BF),
            pltpu.SemaphoreType.DMA((2 * PIECES + 8,)),
        ],
        compiler_params=PARAMS,
        name="step",
    )(fetch_count[0], inputs, m1, wt, back, column, degree1)
    returned = lax.all_to_all(slot_grads, "table", split_axis=0, concat_axis=0, tiled=True)

    node_out, keep, send, send2 = pl.pallas_call(
        grads_kernel,
        out_shape=(
            shaped((seeds, feature), BF),
            shaped((kinds, feature, feature), F32),
            shaped((kinds // 2, feature, feature), BF),
            shaped((kinds // 2, feature, feature), BF),
        ),
        in_specs=[smem] + whole(7),
        out_specs=tuple(whole(4)),
        scratch_shapes=[pltpu.VMEM((feature, kinds * seeds), BF)],
        compiler_params=PARAMS,
        name="grads",
    )(core.reshape(1), agg, hidden, grad_pre, m2, wt, degree2, cot)
    other = jnp.concatenate([lax.ppermute(send, "dp", swap), lax.ppermute(send2, "dp", swap)])
    half = (keep + other.astype(F32)).astype(BF).reshape(-1, feature)
    half, returned = lax.optimization_barrier((half, returned))
    share = rows // groups
    keep_rows, give_rows = pl.pallas_call(
        scatter_kernel,
        out_shape=(shaped((rows // 2, feature), F32),) * 2,
        in_specs=[smem] + whole(2),
        out_specs=tuple(whole(2)),
        scratch_shapes=[pltpu.VMEM((rows, slots), BF)],
        compiler_params=ROOMY,
        name="scatter",
    )(lax.axis_index("dp").reshape(1), asked.reshape(1, slots), returned)

    def halve(keep_rows, give_rows, bit):
        got = lax.ppermute(give_rows, "dp", [(i, i ^ bit) for i in range(groups)])
        return keep_rows + got

    scattered = lax.all_to_all(
        half, both, split_axis=0, concat_axis=0, tiled=True, axis_index_groups=planes
    )
    rest = halve(keep_rows, give_rows, 1)
    rest = halve(rest[: rows // 4], rest[rows // 4 :], 2)
    partial = jnp.sum(scattered.reshape(shards, -1, feature).astype(F32), axis=0).astype(BF)
    crossed = lax.all_to_all(
        jnp.broadcast_to(partial[None], (chips,) + partial.shape).reshape(-1, feature),
        both,
        split_axis=0,
        concat_axis=0,
        tiled=True,
        axis_index_groups=lines,
    )
    total = jnp.sum(crossed.reshape(chips, -1, feature).astype(F32), axis=0)
    batch = seeds * groups * shards
    mean = (total / jnp.sqrt(jnp.float32(batch))).astype(BF)
    rest = halve(rest[: rows // 8], rest[rows // 8 :], 4)
    mean, rest = lax.optimization_barrier((mean, rest))
    mine_half = lax.all_to_all(
        jnp.broadcast_to(mean[None], (shards,) + mean.shape).reshape(-1, feature),
        both,
        split_axis=0,
        concat_axis=0,
        tiled=True,
        axis_index_groups=planes,
    ).reshape(kinds, feature, feature)
    table_part = halve(rest[:share], rest[share:], 8)
    mine_half, table_part = lax.optimization_barrier((mine_half, table_part))
    other_half = lax.ppermute(mine_half, "dp", swap)
    weight_grad = pl.pallas_call(
        place_kernel,
        out_shape=shaped(weights.shape, BF),
        in_specs=[smem, far],
        out_specs=far,
        scratch_shapes=[pltpu.SemaphoreType.DMA],
        compiler_params=PARAMS,
        name="place_mine",
    )(core.reshape(1), mine_half)
    weight_grad = pl.pallas_call(
        place_other_kernel,
        out_shape=shaped(weights.shape, BF),
        in_specs=[smem, far, far],
        out_specs=far,
        scratch_shapes=[pltpu.SemaphoreType.DMA],
        input_output_aliases={2: 0},
        compiler_params=PARAMS,
        name="place_other",
    )(1 - core.reshape(1), other_half, weight_grad)
    return (node_out[None, None], weight_grad, table_part[None])


def solution(mesh):
    return jax.shard_map(
        body,
        mesh=mesh,
        in_specs=(
            P("table", None),
            P(),
            P("dp", "table", None, None),
            P("dp", "table", None),
            P("dp", "table", None),
            P("dp", "table", None, None, None),
            P("dp", "table", None, None),
            P("dp", "table", None),
            P("dp", "table", None, None, None),
            P("dp", "table", None, None),
            P("dp", "table", None, None),
        ),
        out_specs=(P("dp", "table", None, None), P(), P("table", "dp", None)),
        check_vma=False,
    )
```

```python
import jax
import jax.numpy as jnp
from jax import lax
from jax.experimental import pallas as pl
from jax.experimental.pallas import tpu as pltpu
from jax.sharding import PartitionSpec as P

BF = jnp.bfloat16
F32 = jnp.float32
PIECES = 4
PARAMS = pltpu.CompilerParams(vmem_limit_bytes=58 * 1024 * 1024)
ROOMY = pltpu.CompilerParams(vmem_limit_bytes=52 * 1024 * 1024)


def dot(a, b):
    return lax.dot_general(a, b, (((1,), (0,)), ((), ())), preferred_element_type=F32)


def dot_nt(a, b):
    return lax.dot_general(a, b, (((1,), (1,)), ((), ())), preferred_element_type=F32)


def two_part(x):
    high = x.astype(BF)
    return high, (x - high.astype(F32)).astype(BF)


def gather_kernel(asked_ref, table_ref, out_ref, hot_ref):
    groups, width = asked_ref.shape
    rows = table_ref.shape[0]
    columns = jnp.transpose(asked_ref[...].astype(F32))
    lanes = lax.broadcasted_iota(jnp.int32, (width, rows), 1).astype(F32)
    for j in range(groups):
        hot_ref[pl.ds(j * width, width), :] = jnp.where(
            lanes == columns[:, j : j + 1], 1.0, 0.0
        ).astype(BF)
    out_ref[...] = dot(hot_ref[...], table_ref[...]).astype(BF)


def counts_of(selfs, edges_ref, degree_ref, out_ref, height):
    relations, fan, nodes = edges_ref.shape
    slots = lax.broadcasted_iota(jnp.int32, (height, nodes), 0)
    out_ref[:, 0:nodes] = jnp.where(slots == selfs, 1.0, 0.0).astype(BF)
    for r in range(relations):
        degree = degree_ref[:, r * nodes : (r + 1) * nodes]
        total = None
        for f in range(fan):
            edge = jnp.where(degree > f, edges_ref[r, f : f + 1, :], -1)
            hit = jnp.where(slots == edge, 1.0, 0.0)
            total = hit if total is None else total + hit
        out_ref[:, (r + 1) * nodes : (r + 2) * nodes] = total.astype(BF)


def inverse_columns(degree_ref, relations):
    nodes = degree_ref.shape[1] // relations
    inverse = 1.0 / degree_ref[...].astype(F32)
    rows = [inverse[:, r * nodes : (r + 1) * nodes] for r in range(relations)]
    return jnp.transpose(
        jnp.concatenate(rows + [jnp.ones((8 - relations, nodes), F32)], axis=0)
    )


def prepare_kernel(
    self1_ref,
    edges1_ref,
    degree1_ref,
    self2_ref,
    edges2_ref,
    degree2_ref,
    weights_ref,
    cot_ref,
    m1_ref,
    m2_ref,
    wt_ref,
    back_ref,
    column_ref,
    high_ref,
    low_ref,
):
    counts_of(self1_ref[...], edges1_ref, degree1_ref, m1_ref, m1_ref.shape[0])
    counts_of(self2_ref[...], edges2_ref, degree2_ref, m2_ref, m2_ref.shape[0])
    layers, kinds = weights_ref.shape[0], weights_ref.shape[1]
    for layer in range(layers):
        for r in range(kinds):
            wt_ref[layer, r] = jnp.transpose(weights_ref[layer, r].astype(F32)).astype(BF)
    column_ref[...] = inverse_columns(degree1_ref, edges1_ref.shape[0])
    column2 = inverse_columns(degree2_ref, edges2_ref.shape[0])
    seeds = cot_ref.shape[0]
    cot = cot_ref[...]
    for r in range(kinds):
        part = dot_nt(cot, weights_ref[1, r])
        if r > 0:
            part = part * column2[:, r - 1 : r]
        high, low = two_part(part)
        high_ref[pl.ds(r * seeds, seeds), :] = high
        low_ref[pl.ds(r * seeds, seeds), :] = low
    m2 = m2_ref[...]
    back_ref[...] = jnp.transpose(dot(m2, high_ref[...]) + dot(m2, low_ref[...]))


def step_kernel(
    count_ref,
    x_far,
    m1_far,
    wt_far,
    back_far,
    column_far,
    degree_far,
    slot_far,
    agg_far,
    hidden_far,
    grad_far,
    x_ref,
    m1_ref,
    wt_ref,
    back_ref,
    column_ref,
    degree_ref,
    slot_ref,
    agg_ref,
    hidden_ref,
    grad_ref,
    xt_ref,
    spread_ref,
    sems,
):
    shards = count_ref.shape[1]
    slots, feature = x_ref.shape
    width = slots // shards
    kinds = wt_ref.shape[1]
    nodes = grad_ref.shape[0]
    size = slots // PIECES
    pieces = [pl.ds(n * size, size) for n in range(PIECES)]
    x_loads = [
        pltpu.make_async_copy(x_far.at[part], x_ref.at[part], sems.at[n])
        for n, part in enumerate(pieces)
    ]
    used = PIECES
    blocks = [pl.ds(r * nodes, nodes) for r in range(kinds)]
    m1_loads = [
        pltpu.make_async_copy(m1_far.at[:, block], m1_ref.at[:, block], sems.at[used + r])
        for r, block in enumerate(blocks)
    ]
    used += kinds
    loads = [
        pltpu.make_async_copy(source, target, sems.at[used + n])
        for n, (source, target) in enumerate(
            [
                (wt_far.at[pl.ds(0, 1)], wt_ref),
                (degree_far, degree_ref),
                (back_far, back_ref),
                (column_far, column_ref),
            ]
        )
    ]
    used += len(loads)
    for load in x_loads + m1_loads[:1] + loads + m1_loads[1:]:
        load.start()
    position = lax.broadcasted_iota(jnp.int32, (width, feature), 0)
    per_piece = shards // PIECES
    for n in range(PIECES):
        x_loads[n].wait()
        rows = []
        for k in range(n * per_piece, (n + 1) * per_piece):
            block = x_ref[pl.ds(k * width, width), :].astype(F32)
            rows.append(jnp.where(position < count_ref[0, k], block, 0.0))
        xt_ref[:, pieces[n]] = jnp.transpose(jnp.concatenate(rows, axis=0)).astype(BF)
    for load in loads:
        load.wait()
    xt = xt_ref[...]
    inverse = 1.0 / degree_ref[...].astype(F32)
    pre = None
    for r in range(kinds):
        m1_loads[r].wait()
        part = dot(xt, m1_ref[:, r * nodes : (r + 1) * nodes])
        if r > 0:
            part = part * inverse[:, (r - 1) * nodes : r * nodes]
        part = part.astype(BF)
        agg_ref[:, r * nodes : (r + 1) * nodes] = part
        term = dot(wt_ref[0, r], part)
        pre = term if pre is None else pre + term
    stores = [pltpu.make_async_copy(agg_ref, agg_far, sems.at[used])]
    logistic = 1.0 / (1.0 + jnp.exp(-pre))
    hidden_ref[...] = (pre * logistic).astype(BF)
    stores.append(pltpu.make_async_copy(hidden_ref, hidden_far, sems.at[used + 1]))
    slope = logistic * (1.0 + pre * (1.0 - logistic))
    grad_pre = jnp.transpose(back_ref[...] * slope).astype(BF)
    grad_ref[...] = grad_pre
    stores.append(pltpu.make_async_copy(grad_ref, grad_far, sems.at[used + 2]))
    for store in stores:
        store.start()
    used += len(stores)
    for r in range(kinds):
        part = dot(grad_pre, wt_ref[0, r])
        if r > 0:
            part = part * column_ref[:, r - 1 : r]
        spread_ref[pl.ds(r * nodes, nodes), :] = part.astype(BF)
    spread = spread_ref[...]
    for n in range(PIECES):
        grads = dot(m1_ref[pieces[n], :], spread)
        for k in range(n * per_piece, (n + 1) * per_piece):
            first = (k - n * per_piece) * width
            slot_ref[pl.ds(k * width, width), :] = jnp.where(
                position < count_ref[0, k], grads[first : first + width, :], 0.0
            ).astype(BF)
        store = pltpu.make_async_copy(
            slot_ref.at[pieces[n]], slot_far.at[pieces[n]], sems.at[used + n]
        )
        store.start()
        stores.append(store)
    for store in stores:
        store.wait()


def grads_kernel(
    core_ref,
    agg_ref,
    hidden_ref,
    grad_ref,
    m2_ref,
    wt_ref,
    degree_ref,
    cot_ref,
    node_ref,
    keep_ref,
    send_ref,
    send2_ref,
    agg2_ref,
):
    kinds = wt_ref.shape[1]
    nodes = grad_ref.shape[0]
    seeds = cot_ref.shape[0]
    inverse = 1.0 / degree_ref[...].astype(F32)
    hidden = hidden_ref[...]
    out = None
    for r in range(kinds):
        part = dot(hidden, m2_ref[:, r * seeds : (r + 1) * seeds])
        if r > 0:
            part = part * inverse[:, (r - 1) * seeds : r * seeds]
        part = part.astype(BF)
        agg2_ref[:, r * seeds : (r + 1) * seeds] = part
        term = dot(wt_ref[1, r], part)
        out = term if out is None else out + term
    node_ref[...] = jnp.transpose(out).astype(BF)

    def bottom(r):
        return dot(agg_ref[:, r * nodes : (r + 1) * nodes], grad_ref[...])

    def top(r):
        return dot(agg2_ref[:, r * seeds : (r + 1) * seeds], cot_ref[...])

    def send(r, value):
        half = send_ref.shape[0]
        if r < half:
            send_ref[r] = value
        else:
            send2_ref[r - half] = value

    @pl.when(core_ref[0] == 0)
    def first():
        for r in range(kinds):
            keep_ref[r] = bottom(r)
            send(r, top(r).astype(BF))

    @pl.when(core_ref[0] != 0)
    def second():
        for r in range(kinds):
            keep_ref[r] = top(r)
            send(r, bottom(r).astype(BF))


def scatter_kernel(me_ref, asked_ref, grads_ref, keep_ref, give_ref, hot_ref):
    blocks = 16
    rows, slots = hot_ref.shape
    share = rows // blocks
    half = rows // 2
    asked = asked_ref[...]
    within = lax.broadcasted_iota(jnp.int32, (share, slots), 0)
    for b in range(blocks):
        flip = sum(((b >> n) & 1) << (3 - n) for n in range(4))
        index = within + (me_ref[0] ^ flip) * share
        hot_ref[pl.ds(b * share, share), :] = jnp.where(index == asked, 1.0, 0.0).astype(BF)
    grads = grads_ref[...]
    give_ref[...] = dot(hot_ref[half:, :], grads)
    keep_ref[...] = dot(hot_ref[:half, :], grads)


def whole(n):
    return [pl.BlockSpec(memory_space=pltpu.VMEM)] * n


def shaped(shape, kind):
    return jax.ShapeDtypeStruct(shape, kind)


def body(
    table,
    weights,
    fetch_rows,
    fetch_count,
    first_self,
    first_edges,
    first_degree,
    second_self,
    second_edges,
    second_degree,
    cotangent,
):
    wanted = fetch_rows[0, 0]
    shards, width = wanted.shape
    rows, feature = table.shape
    slots = shards * width
    kinds = weights.shape[1]
    nodes = first_self.shape[2]
    seeds = second_self.shape[2]
    groups = lax.axis_size("dp")
    chips = groups // 2
    core = lax.axis_index("dp") % 2
    swap = [(i, i ^ 1) for i in range(groups)]
    both = ("dp", "table")
    down = 8
    across = shards // down

    def device(z, c, y, x):
        return ((z * 2 + c) * down + y) * across + x

    planes = [
        [device(z, 0, y, x) for y in range(down) for x in range(across)] for z in range(chips)
    ] + [[device(z, 1, y, x) for z in range(chips) for x in range(across)] for y in range(down)]

    lines = [
        [device(z, 0, y, x) for z in range(chips)] for y in range(down) for x in range(across)
    ] + [[device(z, 1, y, x) for y in range(down)] for z in range(chips) for x in range(across)]
    far = pl.BlockSpec(memory_space=pl.ANY)
    smem = pl.BlockSpec(memory_space=pltpu.SMEM)

    asked = lax.all_to_all(wanted, "table", split_axis=0, concat_axis=0, tiled=True)

    degree1 = first_degree.reshape(1, -1)
    degree2 = second_degree.reshape(1, -1)
    cot = cotangent[0, 0]
    m1, m2, wt, back, column = pl.pallas_call(
        prepare_kernel,
        out_shape=(
            shaped((slots, kinds * nodes), BF),
            shaped((nodes, kinds * seeds), BF),
            shaped(weights.shape, BF),
            shaped((feature, nodes), F32),
            shaped((nodes, 8), F32),
        ),
        in_specs=whole(8),
        out_specs=tuple(whole(5)),
        scratch_shapes=[
            pltpu.VMEM((kinds * seeds, feature), BF),
            pltpu.VMEM((kinds * seeds, feature), BF),
        ],
        compiler_params=PARAMS,
        name="prepare",
    )(
        first_self[0],
        jnp.swapaxes(first_edges[0, 0], 1, 2),
        degree1,
        second_self[0],
        jnp.swapaxes(second_edges[0, 0], 1, 2),
        degree2,
        weights,
        cot,
    )

    found = pl.pallas_call(
        gather_kernel,
        out_shape=shaped((slots, feature), BF),
        in_specs=whole(2),
        out_specs=whole(1)[0],
        scratch_shapes=[pltpu.VMEM((slots, rows), BF)],
        compiler_params=ROOMY,
        name="gather",
    )(asked, table)
    inputs = lax.all_to_all(found, "table", split_axis=0, concat_axis=0, tiled=True)

    slot_grads, agg, hidden, grad_pre = pl.pallas_call(
        step_kernel,
        out_shape=(
            shaped((slots, feature), BF),
            shaped((feature, kinds * nodes), BF),
            shaped((feature, nodes), BF),
            shaped((nodes, feature), BF),
        ),
        in_specs=[smem] + [far] * 6,
        out_specs=(far,) * 4,
        scratch_shapes=[
            pltpu.VMEM((slots, feature), BF),
            pltpu.VMEM((slots, kinds * nodes), BF),
            pltpu.VMEM((1, kinds, feature, feature), BF),
            pltpu.VMEM((feature, nodes), F32),
            pltpu.VMEM((nodes, 8), F32),
            pltpu.VMEM(degree1.shape, jnp.int32),
            pltpu.VMEM((slots, feature), BF),
            pltpu.VMEM((feature, kinds * nodes), BF),
            pltpu.VMEM((feature, nodes), BF),
            pltpu.VMEM((nodes, feature), BF),
            pltpu.VMEM((feature, slots), BF),
            pltpu.VMEM((kinds * nodes, feature), BF),
            pltpu.SemaphoreType.DMA((2 * PIECES + kinds + 7,)),
        ],
        compiler_params=PARAMS,
        name="step",
    )(fetch_count[0], inputs, m1, wt, back, column, degree1)
    returned = lax.all_to_all(slot_grads, "table", split_axis=0, concat_axis=0, tiled=True)

    node_out, keep, send, send2 = pl.pallas_call(
        grads_kernel,
        out_shape=(
            shaped((seeds, feature), BF),
            shaped((kinds, feature, feature), F32),
            shaped((kinds // 2, feature, feature), BF),
            shaped((kinds // 2, feature, feature), BF),
        ),
        in_specs=[smem] + whole(7),
        out_specs=tuple(whole(4)),
        scratch_shapes=[pltpu.VMEM((feature, kinds * seeds), BF)],
        compiler_params=PARAMS,
        name="grads",
    )(core.reshape(1), agg, hidden, grad_pre, m2, wt, degree2, cot)
    other = jnp.concatenate([lax.ppermute(send, "dp", swap), lax.ppermute(send2, "dp", swap)])
    half = (keep + other.astype(F32)).astype(BF).reshape(-1, feature)
    half, returned = lax.optimization_barrier((half, returned))
    share = rows // groups
    keep_rows, give_rows = pl.pallas_call(
        scatter_kernel,
        out_shape=(shaped((rows // 2, feature), F32),) * 2,
        in_specs=[smem] + whole(2),
        out_specs=tuple(whole(2)),
        scratch_shapes=[pltpu.VMEM((rows, slots), BF)],
        compiler_params=ROOMY,
        name="scatter",
    )(lax.axis_index("dp").reshape(1), asked.reshape(1, slots), returned)

    def halve(keep_rows, give_rows, bit):
        got = lax.ppermute(give_rows, "dp", [(i, i ^ bit) for i in range(groups)])
        return keep_rows + got

    scattered = lax.all_to_all(
        half, both, split_axis=0, concat_axis=0, tiled=True, axis_index_groups=planes
    )
    rest = halve(keep_rows, give_rows, 1)
    rest = halve(rest[: rows // 4], rest[rows // 4 :], 2)
    partial = jnp.sum(scattered.reshape(shards, -1, feature).astype(F32), axis=0).astype(BF)
    crossed = lax.all_to_all(
        jnp.broadcast_to(partial[None], (chips,) + partial.shape).reshape(-1, feature),
        both,
        split_axis=0,
        concat_axis=0,
        tiled=True,
        axis_index_groups=lines,
    )
    total = jnp.sum(crossed.reshape(chips, -1, feature).astype(F32), axis=0)
    batch = seeds * groups * shards
    mean = (total / jnp.sqrt(jnp.float32(batch))).astype(BF)
    rest = halve(rest[: rows // 8], rest[rows // 8 :], 4)
    mean, rest = lax.optimization_barrier((mean, rest))
    mine_half = lax.all_to_all(
        jnp.broadcast_to(mean[None], (shards,) + mean.shape).reshape(-1, feature),
        both,
        split_axis=0,
        concat_axis=0,
        tiled=True,
        axis_index_groups=planes,
    ).reshape(kinds, feature, feature)
    table_part = halve(rest[:share], rest[share:], 8)
    mine_half, table_part = lax.optimization_barrier((mine_half, table_part))
    other_half = lax.ppermute(mine_half, "dp", swap)
    weight_grad = jnp.stack(
        [
            jnp.where(core == 0, mine_half, other_half),
            jnp.where(core == 0, other_half, mine_half),
        ]
    )
    return (node_out[None, None], weight_grad, table_part[None])


def solution(mesh):
    return jax.shard_map(
        body,
        mesh=mesh,
        in_specs=(
            P("table", None),
            P(),
            P("dp", "table", None, None),
            P("dp", "table", None),
            P("dp", "table", None),
            P("dp", "table", None, None, None),
            P("dp", "table", None, None),
            P("dp", "table", None),
            P("dp", "table", None, None, None),
            P("dp", "table", None, None),
            P("dp", "table", None, None),
        ),
        out_specs=(P("dp", "table", None, None), P(), P("table", "dp", None)),
        check_vma=False,
    )
```

```python
import jax
import jax.numpy as jnp
from jax import lax
from jax.experimental import pallas as pl
from jax.experimental.pallas import tpu as pltpu
from jax.sharding import PartitionSpec as P

BF = jnp.bfloat16
F32 = jnp.float32
PARAMS = pltpu.CompilerParams(vmem_limit_bytes=52 * 1024 * 1024)


def dot(a, b):
    return lax.dot_general(a, b, (((1,), (0,)), ((), ())), preferred_element_type=F32)


def dot_nt(a, b):
    return lax.dot_general(a, b, (((1,), (1,)), ((), ())), preferred_element_type=F32)


def two_part(x):
    high = x.astype(BF)
    return high, (x - high.astype(F32)).astype(BF)


def gather_kernel(asked_ref, table_ref, out_ref, hot_ref):
    groups, width = asked_ref.shape
    rows = table_ref.shape[0]
    columns = jnp.transpose(asked_ref[...].astype(F32))
    lanes = lax.broadcasted_iota(jnp.int32, (width, rows), 1).astype(F32)
    for j in range(groups):
        hot_ref[pl.ds(j * width, width), :] = jnp.where(
            lanes == columns[:, j : j + 1], 1.0, 0.0
        ).astype(BF)
    out_ref[...] = dot(hot_ref[...], table_ref[...]).astype(BF)


def counts_of(selfs, edges_ref, degree_ref, out_ref, slots):
    relations, fan, nodes = edges_ref.shape
    out_ref[:, 0:nodes] = jnp.where(slots == selfs, 1.0, 0.0).astype(BF)
    for r in range(relations):
        degree = degree_ref[:, r * nodes : (r + 1) * nodes]
        total = None
        for f in range(fan):
            edge = jnp.where(degree > f, edges_ref[r, f : f + 1, :], -1)
            hit = jnp.where(slots == edge, 1.0, 0.0)
            total = hit if total is None else total + hit
        out_ref[:, (r + 1) * nodes : (r + 2) * nodes] = total.astype(BF)


def inverse_rows(degree_ref, relations):
    nodes = degree_ref.shape[1] // relations
    inverse = 1.0 / degree_ref[...].astype(F32)
    rows = [inverse[:, r * nodes : (r + 1) * nodes] for r in range(relations)]
    return jnp.concatenate(rows + [jnp.ones((8 - relations, nodes), F32)], axis=0)


def prepare_kernel(
    count_ref,
    self1_ref,
    edges1_ref,
    degree1_ref,
    self2_ref,
    edges2_ref,
    degree2_ref,
    weights_ref,
    cot_ref,
    m1_ref,
    m2_ref,
    wt_ref,
    extra_ref,
    high_ref,
    low_ref,
):
    shards = count_ref.shape[1]
    width = m1_ref.shape[0] // shards
    nodes = self1_ref.shape[1]
    position = lax.broadcasted_iota(jnp.int32, (width, nodes), 0)
    live = [
        jnp.where(position < count_ref[0, k], position + k * width, -2) for k in range(shards)
    ]
    counts_of(
        self1_ref[...], edges1_ref, degree1_ref, m1_ref, jnp.concatenate(live, axis=0)
    )
    second = lax.broadcasted_iota(jnp.int32, (m2_ref.shape[0], self2_ref.shape[1]), 0)
    counts_of(self2_ref[...], edges2_ref, degree2_ref, m2_ref, second)
    layers, kinds = weights_ref.shape[0], weights_ref.shape[1]
    for layer in range(layers):
        for r in range(kinds):
            wt_ref[layer, r] = jnp.transpose(weights_ref[layer, r].astype(F32)).astype(BF)
    inverse1 = inverse_rows(degree1_ref, edges1_ref.shape[0])
    extra_ref[nodes : nodes + 8, 0:nodes] = inverse1
    extra_ref[0:nodes, nodes : nodes + 8] = jnp.transpose(inverse1)
    column2 = jnp.transpose(inverse_rows(degree2_ref, edges2_ref.shape[0]))
    seeds = cot_ref.shape[0]
    cot = cot_ref[...]
    for r in range(kinds):
        part = dot_nt(cot, weights_ref[1, r])
        if r > 0:
            part = part * column2[:, r - 1 : r]
        high, low = two_part(part)
        high_ref[pl.ds(r * seeds, seeds), :] = high
        low_ref[pl.ds(r * seeds, seeds), :] = low
    m2 = m2_ref[...]
    extra_ref[0:nodes, 0:nodes] = jnp.transpose(dot(m2, high_ref[...]) + dot(m2, low_ref[...]))


def step_kernel(
    x_ref, m1_far, wt_far, extra_ref, slot_ref, all_ref, spread_ref, m1_ref, wt_ref, sems
):
    copies = [
        pltpu.make_async_copy(m1_far, m1_ref, sems.at[0]),
        pltpu.make_async_copy(wt_far.at[pl.ds(0, 1)], wt_ref, sems.at[1]),
    ]
    for copy in copies:
        copy.start()
    kinds = wt_ref.shape[1]
    nodes = all_ref.shape[0]
    xt = jnp.transpose(x_ref[...])
    for copy in copies:
        copy.wait()
    pre = None
    for r in range(kinds):
        part = dot(xt, m1_ref[:, r * nodes : (r + 1) * nodes])
        if r > 0:
            part = part * extra_ref[nodes + r - 1 : nodes + r, 0:nodes]
        part = part.astype(BF)
        all_ref[:, r * nodes : (r + 1) * nodes] = part
        term = dot(wt_ref[0, r], part)
        pre = term if pre is None else pre + term
    logistic = 1.0 / (1.0 + jnp.exp(-pre))
    all_ref[:, kinds * nodes : (kinds + 1) * nodes] = (pre * logistic).astype(BF)
    slope = logistic * (1.0 + pre * (1.0 - logistic))
    grad_pre = jnp.transpose(extra_ref[0:nodes, 0:nodes] * slope).astype(BF)
    all_ref[:, (kinds + 1) * nodes : (kinds + 2) * nodes] = grad_pre
    for r in range(kinds):
        part = dot(grad_pre, wt_ref[0, r])
        if r > 0:
            part = part * extra_ref[0:nodes, nodes + r - 1 : nodes + r]
        spread_ref[pl.ds(r * nodes, nodes), :] = part.astype(BF)
    slot_ref[...] = dot(m1_ref[...], spread_ref[...]).astype(BF)


def grads_kernel(
    core_ref,
    all_ref,
    m2_ref,
    wt_ref,
    degree_ref,
    cot_ref,
    node_ref,
    keep_ref,
    send_ref,
    send2_ref,
    agg2_ref,
):
    kinds = wt_ref.shape[1]
    nodes = all_ref.shape[0]
    seeds = cot_ref.shape[0]
    inverse = 1.0 / degree_ref[...].astype(F32)
    hidden = all_ref[:, kinds * nodes : (kinds + 1) * nodes]
    grad_pre = all_ref[:, (kinds + 1) * nodes : (kinds + 2) * nodes]
    out = None
    for r in range(kinds):
        part = dot(hidden, m2_ref[:, r * seeds : (r + 1) * seeds])
        if r > 0:
            part = part * inverse[:, (r - 1) * seeds : r * seeds]
        part = part.astype(BF)
        agg2_ref[:, r * seeds : (r + 1) * seeds] = part
        term = dot(wt_ref[1, r], part)
        out = term if out is None else out + term
    node_ref[...] = jnp.transpose(out).astype(BF)

    def bottom(r):
        return dot(all_ref[:, r * nodes : (r + 1) * nodes], grad_pre)

    def top(r):
        return dot(agg2_ref[:, r * seeds : (r + 1) * seeds], cot_ref[...])

    def send(r, value):
        half = send_ref.shape[0]
        if r < half:
            send_ref[r] = value
        else:
            send2_ref[r - half] = value

    @pl.when(core_ref[0] == 0)
    def first():
        for r in range(kinds):
            keep_ref[r] = bottom(r)
            send(r, top(r).astype(BF))

    @pl.when(core_ref[0] != 0)
    def second():
        for r in range(kinds):
            keep_ref[r] = top(r)
            send(r, bottom(r).astype(BF))


def scatter_kernel(me_ref, asked_ref, grads_ref, keep_ref, give_ref, hot_ref):
    blocks = 16
    rows, slots = hot_ref.shape
    share = rows // blocks
    half = rows // 2
    asked = asked_ref[...]
    within = lax.broadcasted_iota(jnp.int32, (share, slots), 0)
    for b in range(blocks):
        flip = sum(((b >> n) & 1) << (3 - n) for n in range(4))
        index = within + (me_ref[0] ^ flip) * share
        hot_ref[pl.ds(b * share, share), :] = jnp.where(index == asked, 1.0, 0.0).astype(BF)
    grads = grads_ref[...]
    give_ref[...] = dot(hot_ref[half:, :], grads)
    keep_ref[...] = dot(hot_ref[:half, :], grads)


def whole(n):
    return [pl.BlockSpec(memory_space=pltpu.VMEM)] * n


def shaped(shape, kind):
    return jax.ShapeDtypeStruct(shape, kind)


def body(
    table,
    weights,
    fetch_rows,
    fetch_count,
    first_self,
    first_edges,
    first_degree,
    second_self,
    second_edges,
    second_degree,
    cotangent,
):
    wanted = fetch_rows[0, 0]
    shards, width = wanted.shape
    rows, feature = table.shape
    slots = shards * width
    kinds = weights.shape[1]
    nodes = first_self.shape[2]
    seeds = second_self.shape[2]
    groups = lax.axis_size("dp")
    chips = groups // 2
    core = lax.axis_index("dp") % 2
    swap = [(i, i ^ 1) for i in range(groups)]
    both = ("dp", "table")
    down = 8
    across = shards // down

    def device(z, c, y, x):
        return ((z * 2 + c) * down + y) * across + x

    planes = [
        [device(z, 0, y, x) for y in range(down) for x in range(across)] for z in range(chips)
    ] + [[device(z, 1, y, x) for z in range(chips) for x in range(across)] for y in range(down)]

    lines = [
        [device(z, 0, y, x) for z in range(chips)] for y in range(down) for x in range(across)
    ] + [[device(z, 1, y, x) for y in range(down)] for z in range(chips) for x in range(across)]
    far = pl.BlockSpec(memory_space=pl.ANY)
    smem = pl.BlockSpec(memory_space=pltpu.SMEM)

    asked = lax.all_to_all(wanted, "table", split_axis=0, concat_axis=0, tiled=True)

    degree1 = first_degree.reshape(1, -1)
    degree2 = second_degree.reshape(1, -1)
    cot = cotangent[0, 0]
    m1, m2, wt, extra = pl.pallas_call(
        prepare_kernel,
        out_shape=(
            shaped((slots, kinds * nodes), BF),
            shaped((nodes, kinds * seeds), BF),
            shaped(weights.shape, BF),
            shaped((nodes + 8, nodes + 128), F32),
        ),
        in_specs=[smem] + whole(8),
        out_specs=tuple(whole(4)),
        scratch_shapes=[
            pltpu.VMEM((kinds * seeds, feature), BF),
            pltpu.VMEM((kinds * seeds, feature), BF),
        ],
        compiler_params=PARAMS,
        name="prepare",
    )(
        fetch_count[0],
        first_self[0],
        jnp.swapaxes(first_edges[0, 0], 1, 2),
        degree1,
        second_self[0],
        jnp.swapaxes(second_edges[0, 0], 1, 2),
        degree2,
        weights,
        cot,
    )

    found = pl.pallas_call(
        gather_kernel,
        out_shape=shaped((slots, feature), BF),
        in_specs=whole(2),
        out_specs=whole(1)[0],
        scratch_shapes=[pltpu.VMEM((slots, rows), BF)],
        compiler_params=PARAMS,
        name="gather",
    )(asked, table)
    inputs = lax.all_to_all(found, "table", split_axis=0, concat_axis=0, tiled=True)

    slot_grads, packed = pl.pallas_call(
        step_kernel,
        out_shape=(
            shaped((slots, feature), BF),
            shaped((nodes, (kinds + 2) * nodes), BF),
        ),
        in_specs=whole(1) + [far] * 2 + whole(1),
        out_specs=tuple(whole(2)),
        scratch_shapes=[
            pltpu.VMEM((kinds * nodes, feature), BF),
            pltpu.VMEM((slots, kinds * nodes), BF),
            pltpu.VMEM((1, kinds, feature, feature), BF),
            pltpu.SemaphoreType.DMA((2,)),
        ],
        compiler_params=PARAMS,
        name="step",
    )(inputs, m1, wt, extra)
    returned = lax.all_to_all(slot_grads, "table", split_axis=0, concat_axis=0, tiled=True)

    node_out, keep, send, send2 = pl.pallas_call(
        grads_kernel,
        out_shape=(
            shaped((seeds, feature), BF),
            shaped((kinds, feature, feature), F32),
            shaped((kinds // 2, feature, feature), BF),
            shaped((kinds // 2, feature, feature), BF),
        ),
        in_specs=[smem] + whole(5),
        out_specs=tuple(whole(4)),
        scratch_shapes=[pltpu.VMEM((feature, kinds * seeds), BF)],
        compiler_params=PARAMS,
        name="grads",
    )(core.reshape(1), packed, m2, wt, degree2, cot)
    other = jnp.concatenate([lax.ppermute(send, "dp", swap), lax.ppermute(send2, "dp", swap)])
    half = (keep + other.astype(F32)).astype(BF).reshape(-1, feature)
    half, returned = lax.optimization_barrier((half, returned))
    share = rows // groups
    keep_rows, give_rows = pl.pallas_call(
        scatter_kernel,
        out_shape=(shaped((rows // 2, feature), F32),) * 2,
        in_specs=[smem] + whole(2),
        out_specs=tuple(whole(2)),
        scratch_shapes=[pltpu.VMEM((rows, slots), BF)],
        compiler_params=PARAMS,
        name="scatter",
    )(lax.axis_index("dp").reshape(1), asked.reshape(1, slots), returned)

    def halve(keep_rows, give_rows, bit):
        got = lax.ppermute(give_rows, "dp", [(i, i ^ bit) for i in range(groups)])
        return keep_rows + got

    scattered = lax.all_to_all(
        half, both, split_axis=0, concat_axis=0, tiled=True, axis_index_groups=planes
    )
    rest = halve(keep_rows, give_rows, 1)
    rest = halve(rest[: rows // 4], rest[rows // 4 :], 2)
    partial = jnp.sum(scattered.reshape(shards, -1, feature).astype(F32), axis=0).astype(BF)
    crossed = lax.all_to_all(
        jnp.broadcast_to(partial[None], (chips,) + partial.shape).reshape(-1, feature),
        both,
        split_axis=0,
        concat_axis=0,
        tiled=True,
        axis_index_groups=lines,
    )
    total = jnp.sum(crossed.reshape(chips, -1, feature).astype(F32), axis=0)
    batch = seeds * groups * shards
    mean = (total / jnp.sqrt(jnp.float32(batch))).astype(BF)
    rest = halve(rest[: rows // 8], rest[rows // 8 :], 4)
    mean, rest = lax.optimization_barrier((mean, rest))
    mine_half = lax.all_to_all(
        jnp.broadcast_to(mean[None], (shards,) + mean.shape).reshape(-1, feature),
        both,
        split_axis=0,
        concat_axis=0,
        tiled=True,
        axis_index_groups=planes,
    ).reshape(kinds, feature, feature)
    table_part = halve(rest[:share], rest[share:], 8)
    mine_half, table_part = lax.optimization_barrier((mine_half, table_part))
    other_half = lax.ppermute(mine_half, "dp", swap)
    weight_grad = jnp.stack(
        [
            jnp.where(core == 0, mine_half, other_half),
            jnp.where(core == 0, other_half, mine_half),
        ]
    )
    return (node_out[None, None], weight_grad, table_part[None])


def solution(mesh):
    return jax.shard_map(
        body,
        mesh=mesh,
        in_specs=(
            P("table", None),
            P(),
            P("dp", "table", None, None),
            P("dp", "table", None),
            P("dp", "table", None),
            P("dp", "table", None, None, None),
            P("dp", "table", None, None),
            P("dp", "table", None),
            P("dp", "table", None, None, None),
            P("dp", "table", None, None),
            P("dp", "table", None, None),
        ),
        out_specs=(P("dp", "table", None, None), P(), P("table", "dp", None)),
        check_vma=False,
    )
```
